256 devices in a mesh: seq: 64 (over z_hi, y, x, core), head: 4 (over z_lo).
Axes of the slice: x: 4, y: 4, z: 8 (z_hi: 2, z_lo: 4; z = z_hi * 4 + z_lo), core: 2. Of those that a mesh axis runs over, the one named last changes fastest.
Arguments:
- queries: bfloat16 [64, 64, 192], P('seq', 'head'), may hold values from -120 to 120
- new_latent: bfloat16 [64, 576], P('seq'), may hold values from -6 to 6
- cache: bfloat16 [16, 8192, 576], P('head', 'seq'), may hold values from -6 to 6
- lengths: int32 [16], replicated, may hold values from 8 to 8192, as said below
- w_uk: bfloat16 [64, 128, 512], P('head'), may hold values from -0.5 to 0.5
- w_uv: bfloat16 [64, 512, 128], P('head'), may hold values from -0.25 to 0.25
Outputs:
- attended: bfloat16 [64, 64, 128], P('seq', 'head')
The draws below stay inside these ranges and needn't reach their ends.
Inputs may be any that keep to these rules, and one draw needn't show every extreme that they name: `lengths`: each sequence keeps at least 8 cached slots; some sequence has exactly 8192.
All inputs are finite; a program needn't handle non-finite values.
Results may differ from the reference program's by a relative error of at most 0.039.
Values may be sent and summed in bfloat16 or wider, within the bound.
A program may use at most 64 MiB of HBM per device.

```python
import jax
import jax.numpy as jnp
from jax import lax

HEADS = 64
NOPE = 128
ROPE = 64
LATENT = 512
VDIM = 128
SPEC = 4
SEQS = 16
CACHE_LEN = 8192
ROWS = 64


def draw_queries(key, part):
    shape = (ROWS, HEADS, NOPE + ROPE)
    values = jnp.clip(jax.random.normal(jax.random.fold_in(key, 32), shape, jnp.float32), -5.0, 5.0)
    return values.astype(jnp.bfloat16)


def draw_cache(key, part):
    shape = (SEQS, CACHE_LEN, LATENT + ROPE)
    values = jnp.clip(jax.random.normal(jax.random.fold_in(key, 42), shape, jnp.float32), -5.0, 5.0)
    return values.astype(jnp.bfloat16)


def draw_lengths(key, part):
    drawn = jax.random.randint(jax.random.fold_in(key, 21), (SEQS,), 8, CACHE_LEN + 1)
    longest = jax.random.randint(jax.random.fold_in(key, 22), (), 0, SEQS)
    return drawn.at[longest].set(CACHE_LEN).astype(jnp.int32)


def block_levels(own_key, dims, split, least, top_value):
    loudness, own = 1.0, jax.random.fold_in(own_key, 6)
    for position, blocks in split:
        draws = jnp.exp(jax.random.uniform(jax.random.fold_in(own, position), (blocks,), jnp.float32, least / len(split), top_value / len(split)))
        loudness = loudness * jnp.repeat(draws, dims[position] // blocks).reshape([-1 if axis == position else 1 for axis in range(len(dims))])
    return loudness


def gaussian(own_key, extent, width, bound, cuts=(), kind=jnp.bfloat16):
    result = width * jax.random.normal(own_key, extent, jnp.float32)
    if cuts:
        result = result * block_levels(own_key, extent, cuts, -0.22, 0.18)
    return jnp.clip(result, -bound, bound).astype(kind)


def setup_inputs(seed: int = 0) -> dict:
    streams_of = jax.random.split(jax.random.key(seed), 7)
    return {
        "queries": draw_queries(jax.random.fold_in(streams_of[6], 71), 0),
        "new_latent": gaussian(streams_of[1], (ROWS, LATENT + ROPE), 1.0, 6.0, ((0, 64),)),
        "cache": draw_cache(jax.random.fold_in(streams_of[6], 71), 0),
        "lengths": draw_lengths(jax.random.fold_in(streams_of[6], 71), 0),
        "w_uk": gaussian(streams_of[4], (HEADS, NOPE, LATENT), NOPE ** -0.5, 0.5, ((0, 4),)),
        "w_uv": gaussian(streams_of[5], (HEADS, LATENT, VDIM), LATENT ** -0.5, 0.25, ((0, 4),)),
    }


masked_value = -1.0e30


def reference(queries, new_latent, cache, lengths, w_uk, w_uv):
    row_count, head_count, _ = queries.shape
    q_nope = queries[:, :, :NOPE].astype(jnp.float32)
    absorbed = jnp.einsum("rhn,hnc->rhc", q_nope, w_uk.astype(jnp.float32)).astype(jnp.bfloat16)
    q_full = jnp.concatenate([absorbed, queries[:, :, NOPE:]], axis=2)
    q_seq = q_full.reshape(SEQS, SPEC * head_count, LATENT + ROPE)
    new_seq = new_latent.reshape(SEQS, SPEC, LATENT + ROPE)
    score_scale = (NOPE + ROPE) ** -0.5

    def one_sequence(packed):
        query_tile_block, key_tile_block, incoming_keys, length = packed
        scores = jnp.dot(query_tile_block, key_tile_block.T, preferred_element_type=jnp.float32) * score_scale
        visible = jnp.arange(key_tile_block.shape[0], dtype=jnp.int32)[None, :] < length
        fresh_scores = jnp.dot(query_tile_block, incoming_keys.T, preferred_element_type=jnp.float32) * score_scale
        row_spec = jnp.arange(SPEC * head_count, dtype=jnp.int32)[:, None] // head_count
        causal = jnp.arange(SPEC, dtype=jnp.int32)[None, :] <= row_spec
        row_top = jnp.maximum(jnp.max(jnp.where(visible, scores, masked_value), axis=1),
                              jnp.max(jnp.where(causal, fresh_scores, masked_value), axis=1))
        weights = jnp.where(visible, jnp.exp(scores - row_top[:, None]), 0.0)
        fresh_weights = jnp.where(causal, jnp.exp(fresh_scores - row_top[:, None]), 0.0)
        running_totals = jnp.sum(weights, axis=1) + jnp.sum(fresh_weights, axis=1)
        weighted = jnp.dot(weights.astype(jnp.bfloat16), key_tile_block[:, :LATENT], preferred_element_type=jnp.float32)
        weighted = weighted + jnp.dot(fresh_weights.astype(jnp.bfloat16), incoming_keys[:, :LATENT], preferred_element_type=jnp.float32)
        return weighted / running_totals[:, None]

    latent_output = lax.map(one_sequence, (q_seq, cache, new_seq, lengths))
    latent_output = latent_output.reshape(row_count, head_count, LATENT)
    return jnp.einsum("rhc,hcv->rhv", latent_output, w_uv.astype(jnp.float32),
                      precision=lax.Precision.HIGHEST).astype(jnp.bfloat16)
```

```python
import jax
import jax.numpy as jnp
from jax import lax
from jax.experimental import pallas as pl
from jax.experimental.pallas import tpu as pltpu
from jax.sharding import PartitionSpec as P

NOPE = 128
ROPE = 64
LATENT = 512
WIDTH = LATENT + ROPE
VDIM = 128
SPEC = 4
GROUP = 16
HEADS = 64
SLOTS = 128
NEG = -1e30
SCALE = (NOPE + ROPE) ** -0.5
MESH = pl.DeviceIdType.MESH
F32 = jnp.float32
BF16 = jnp.bfloat16


def dot(a, b, dims):
    return lax.dot_general(a, b, (dims, ((), ())), preferred_element_type=F32)


def kernel(
    q_hbm, nl_hbm, cache_hbm, len_ref, wuk_hbm, wuv_hbm, out_ref,
    wuk, wuv, q_in, nl, kt, kv, q_own, q_all, acc, o_out, s_out, o_in, s_in,
    r_out, t_out, r_in, t_in,
    local_sem, swap_send, swap_recv, nl_send, nl_recv, a_send, a_recv, b_send, b_recv,
    o_send, o_recv, s_send, s_recv, r_send, r_recv, t_send, t_recv,
):
    seq, head = lax.axis_index("seq"), lax.axis_index("head")
    core = lax.rem(seq, 2)
    x = lax.rem(lax.div(seq, 2), 4)
    y = lax.rem(lax.div(seq, 8), 4)
    zhi = lax.div(seq, 32)

    def at(zhi_, y_, x_, core_):
        return ((zhi_ * 4 + y_) * 4 + x_) * 2 + core_

    to_head, to_core = zhi * 2 + lax.div(y, 2), lax.rem(y, 2)
    plane = zhi * 4 + y
    from_zhi, from_y = lax.div(head, 2), lax.rem(head, 2) * 2 + core
    own_piece = (to_head == head) & (to_core == core)

    def worker(j):
        k = lax.rem(plane + j, 8)
        return (k * 4 + x) * 2 + to_core, to_head

    def owner(j):
        core_ = lax.rem(core + j // 4, 2)
        head_ = lax.rem(head + j % 4, 4)
        return at(from_zhi, from_y, x, core_), head_

    def x_peer(d):
        return at(zhi, y, lax.rem(x + d, 4), core), head

    mate_x = x + 1 - 2 * lax.rem(x, 2)
    mates = [
        (at(zhi, y, x, 1 - core), head),
        (at(zhi, y, mate_x, core), head),
        (at(zhi, y, mate_x, 1 - core), head),
    ]

    barrier = pltpu.get_barrier_semaphore()

    def greet(device):
        pl.semaphore_signal(barrier, inc=1, device_id=device, device_id_type=MESH)

    for j in range(1, 8):
        greet(worker(j))
        greet(owner(j))

    @pl.when(jnp.logical_not(own_piece))
    def _():
        greet(worker(0))
        greet(owner(0))

    for d in (1, 2, 3):
        greet(x_peer(d))
    greet(mates[0])
    greet(mates[2])

    def remote(src, dst, send, recv, device):
        return pltpu.make_async_remote_copy(
            src_ref=src, dst_ref=dst, send_sem=send, recv_sem=recv,
            device_id=device, device_id_type=MESH,
        )

    half = pl.ds(pl.multiple_of(core * SLOTS, SLOTS), SLOTS)
    token = lax.rem(seq, SPEC)

    load_q = pltpu.make_async_copy(q_hbm.at[0], q_in, local_sem.at[0])
    load_wuk = pltpu.make_async_copy(wuk_hbm, wuk, local_sem.at[1])
    load_nl = pltpu.make_async_copy(nl_hbm, nl.at[token], local_sem.at[2])
    load_kt = pltpu.make_async_copy(
        cache_hbm.at[pl.ds(2 * core, 2)], kt.at[:, :, half], local_sem.at[3]
    )
    load_wuv = pltpu.make_async_copy(wuv_hbm, wuv, local_sem.at[4])
    load_q.start()
    load_wuk.start()
    load_nl.start()
    load_kt.start()
    load_wuv.start()

    load_q.wait()
    q = q_in[...]
    row_of = lax.broadcasted_iota(jnp.int32, (GROUP, GROUP * NOPE), 0)
    col_of = lax.broadcasted_iota(jnp.int32, (GROUP, GROUP * NOPE), 1)
    spread = jnp.concatenate([q[:, :NOPE].astype(F32)] * GROUP, axis=1)
    spread = jnp.where(lax.div(col_of, NOPE) == row_of, spread, 0.0).astype(BF16)
    load_wuk.wait()
    absorbed = dot(spread, wuk[...], ((1,), (0,)))
    q_own[:, :LATENT] = absorbed.astype(BF16)
    q_own[:, LATENT:] = q[:, NOPE:]

    pl.semaphore_wait(barrier, jnp.where(own_piece, 19, 21))

    my_slot = core * 4 + head
    my_rows = pl.ds(pl.multiple_of(GROUP * head, GROUP), GROUP)
    my_place = q_all.at[2 * x + core, my_rows]
    for j in range(1, 8):
        remote(q_own, my_place, a_send.at[j], a_recv.at[my_slot], worker(j)).start()

    @pl.when(own_piece)
    def _():
        pltpu.make_async_copy(q_own, my_place, a_recv.at[my_slot]).start()

    @pl.when(jnp.logical_not(own_piece))
    def _():
        remote(q_own, my_place, a_send.at[0], a_recv.at[my_slot], worker(0)).start()

    swap = remote(
        cache_hbm.at[pl.ds(2 * (1 - core), 2)], kt.at[:, :, half],
        swap_send, swap_recv, mates[0],
    )
    swap.start()
    load_nl.wait()
    for k in range(3):
        remote(nl.at[token], nl.at[token], nl_send.at[k], nl_recv.at[token], mates[k]).start()

    load_kt.wait()
    other = pl.ds(pl.multiple_of((1 - core) * SLOTS, SLOTS), SLOTS)
    pltpu.make_async_copy(
        cache_hbm.at[pl.ds(0, 2)], kt.at[:, :, other], swap_recv
    ).wait()
    for s in range(2):
        kv[s] = kt[s].T

    x_rows = pl.ds(2 * x, 2)
    for c in range(2):
        core_ = lax.rem(core + c, 2)
        for g in range(4):
            head_ = lax.rem(head + g, 4)
            pltpu.make_async_copy(
                q_own,
                q_all.at[2 * x + core_, pl.ds(pl.multiple_of(GROUP * head_, GROUP), GROUP)],
                a_recv.at[core_ * 4 + head_],
            ).wait()
    for d in (1, 3, 2):
        remote(
            q_all.at[x_rows], q_all.at[x_rows], b_send.at[d], b_recv.at[d], x_peer(d)
        ).start()

    chip = lax.div(seq, 2)
    first = 4 * head + 2 * core

    def partial_of(x_, s):
        queries = q_all[pl.ds(2 * x_, 2)].reshape(2 * HEADS, WIDTH)
        scores = dot(kv[s], queries, ((1,), (1,))) * SCALE
        position = chip * (2 * SLOTS) + lax.broadcasted_iota(jnp.int32, scores.shape, 0)
        visible = position < len_ref[first + s]
        top = jnp.max(jnp.where(visible, scores, NEG), axis=0, keepdims=True)
        p = jnp.where(visible, jnp.exp(scores - top), 0.0)
        total = jnp.sum(p, axis=0, keepdims=True)
        weighted = dot(kt[s, :LATENT], p.astype(BF16), ((1,), (0,)))
        return top, total, weighted

    sub = lax.broadcasted_iota(jnp.int32, (8, 2 * HEADS), 0)

    def stats(top, total):
        return jnp.where(sub == 0, top, jnp.where(sub == 1, total, 0.0))

    top0, total0, weighted0 = partial_of(x, lax.div(x, 2))
    acc[...] = weighted0
    for d in (1, 3, 2):
        x_ = lax.rem(x + 4 - d, 4)
        rows = pl.ds(2 * x_, 2)
        pltpu.make_async_copy(q_all.at[rows], q_all.at[rows], b_recv.at[d]).wait()
        top, total, weighted = partial_of(x_, lax.div(x_, 2))
        o_out[d] = weighted.astype(BF16)
        s_out[d] = stats(top, total)
        remote(s_out.at[d], s_in.at[d], s_send.at[d], s_recv.at[d], x_peer(4 - d)).start()
        remote(o_out.at[d], o_in.at[d], o_send.at[d], o_recv.at[d], x_peer(4 - d)).start()

    for d in (1, 3, 2):
        pltpu.make_async_copy(s_in.at[d], s_in.at[d], s_recv.at[d]).wait()
        pltpu.make_async_copy(o_in.at[d], o_in.at[d], o_recv.at[d]).wait()
    tops = [top0] + [s_in[d][0:1] for d in (1, 2, 3)]
    top = jnp.maximum(jnp.maximum(tops[0], tops[1]), jnp.maximum(tops[2], tops[3]))
    factors = [jnp.exp(t - top) for t in tops]
    total = total0 * factors[0]
    merged = acc[...] * factors[0]
    for d in (1, 2, 3):
        total = total + s_in[d][1:2] * factors[d]
        merged = merged + o_in[d].astype(F32) * factors[d]
    t_out[...] = stats(top, total)
    r_out[...] = merged.T.astype(BF16)

    def piece(j):
        core_, head_ = lax.rem(core + j // 4, 2), lax.rem(head + j % 4, 4)
        start = pl.multiple_of(HEADS * core_ + GROUP * head_, GROUP)
        return r_out.at[pl.ds(start, GROUP)]

    def send_to_owner(j):
        return (
            remote(t_out, t_in.at[plane], t_send.at[j], t_recv.at[plane], owner(j)),
            remote(piece(j), r_in.at[plane], r_send.at[j], r_recv.at[plane], owner(j)),
        )

    for j in range(1, 8):
        a, b = send_to_owner(j)
        a.start()
        b.start()

    @pl.when(own_piece)
    def _():
        pltpu.make_async_copy(t_out, t_in.at[plane], t_recv.at[plane]).start()
        pltpu.make_async_copy(piece(0), r_in.at[plane], r_recv.at[plane]).start()

    @pl.when(jnp.logical_not(own_piece))
    def _():
        a, b = send_to_owner(0)
        a.start()
        b.start()

    for k in range(1, 4):
        other_token = lax.rem(token + k, SPEC)
        pltpu.make_async_copy(nl.at[token], nl.at[other_token], nl_recv.at[other_token]).wait()
    mine = q_own[...].astype(F32)
    fresh, keys = [], []
    for i in range(SPEC):
        key = nl[i].astype(F32)
        score = jnp.sum(mine * key, axis=1, keepdims=True) * SCALE
        fresh.append(jnp.where(i <= token, score, NEG))
        keys.append(key[:, :LATENT])
    f_top = jnp.maximum(jnp.maximum(fresh[0], fresh[1]), jnp.maximum(fresh[2], fresh[3]))
    f_total, f_weighted = 0.0, 0.0
    for i in range(SPEC):
        p = jnp.where(i <= token, jnp.exp(fresh[i] - f_top), 0.0)
        f_total = f_total + p
        f_weighted = f_weighted + p.astype(BF16).astype(F32) * keys[i]

    load_wuv.wait()
    for k in range(8):
        pltpu.make_async_copy(t_in.at[k], t_in.at[k], t_recv.at[k]).wait()
        pltpu.make_async_copy(r_in.at[k], r_in.at[k], r_recv.at[k]).wait()
    lane = lax.broadcasted_iota(jnp.int32, (GROUP, 2 * HEADS), 1)
    mine_lane = lane == (
        HEADS * core + GROUP * head + lax.broadcasted_iota(jnp.int32, (GROUP, 2 * HEADS), 0)
    )

    def column(row):
        return jnp.sum(jnp.where(mine_lane, row, 0.0), axis=1, keepdims=True)

    tops = [column(t_in[k][0:1]) for k in range(8)]
    top = f_top
    for t in tops:
        top = jnp.maximum(top, t)
    f_factor = jnp.exp(f_top - top)
    total = f_total * f_factor
    latent = f_weighted * f_factor
    for k in range(8):
        factor = jnp.exp(tops[k] - top)
        total = total + column(t_in[k][1:2]) * factor
        latent = latent + r_in[k].astype(F32) * factor
    latent = latent / total

    high = latent.astype(BF16).astype(F32)
    both = jnp.concatenate([high, latent - high], axis=0)
    wide = jnp.concatenate([both] * GROUP, axis=1)
    row_of = lax.rem(lax.broadcasted_iota(jnp.int32, wide.shape, 0), GROUP)
    col_of = lax.div(lax.broadcasted_iota(jnp.int32, wide.shape, 1), LATENT)
    wide = jnp.where(row_of == col_of, wide, 0.0).astype(BF16)
    projected = dot(wide, wuv[...], ((1,), (0,)))
    out_ref[0] = (projected[:GROUP] + projected[GROUP:]).astype(BF16)

    for j in range(1, 8):
        remote(q_own, my_place, a_send.at[j], a_recv.at[my_slot], worker(j)).wait_send()
        a, b = send_to_owner(j)
        a.wait_send()
        b.wait_send()

    @pl.when(jnp.logical_not(own_piece))
    def _():
        remote(q_own, my_place, a_send.at[0], a_recv.at[my_slot], worker(0)).wait_send()
        a, b = send_to_owner(0)
        a.wait_send()
        b.wait_send()

    swap.wait_send()
    for k in range(3):
        remote(
            nl.at[token], nl.at[token], nl_send.at[k], nl_recv.at[token], mates[k]
        ).wait_send()
    for d in (1, 2, 3):
        remote(
            q_all.at[x_rows], q_all.at[x_rows], b_send.at[d], b_recv.at[d], x_peer(d)
        ).wait_send()
        remote(s_out.at[d], s_in.at[d], s_send.at[d], s_recv.at[d], x_peer(4 - d)).wait_send()
        remote(o_out.at[d], o_in.at[d], o_send.at[d], o_recv.at[d], x_peer(4 - d)).wait_send()


def shards(queries, new_latent, cache, lengths, w_uk, w_uv):
    anywhere = pl.BlockSpec(memory_space=pl.ANY)
    dma = pltpu.SemaphoreType.DMA
    return pl.pallas_call(
        kernel,
        out_shape=jax.ShapeDtypeStruct((1, GROUP, VDIM), BF16),
        in_specs=[
            anywhere,
            anywhere,
            anywhere,
            pl.BlockSpec(memory_space=pltpu.SMEM),
            anywhere,
            anywhere,
        ],
        out_specs=pl.BlockSpec(memory_space=pltpu.VMEM),
        scratch_shapes=[
            pltpu.VMEM((GROUP * NOPE, LATENT), BF16),
            pltpu.VMEM((GROUP * LATENT, VDIM), BF16),
            pltpu.VMEM((GROUP, NOPE + ROPE), BF16),
            pltpu.VMEM((SPEC, 1, WIDTH), BF16),
            pltpu.VMEM((2, WIDTH, 2 * SLOTS), BF16),
            pltpu.VMEM((2, 2 * SLOTS, WIDTH), BF16),
            pltpu.VMEM((GROUP, WIDTH), BF16),
            pltpu.VMEM((8, HEADS, WIDTH), BF16),
            pltpu.VMEM((LATENT, 2 * HEADS), F32),
            pltpu.VMEM((4, LATENT, 2 * HEADS), BF16),
            pltpu.VMEM((4, 8, 2 * HEADS), F32),
            pltpu.VMEM((4, LATENT, 2 * HEADS), BF16),
            pltpu.VMEM((4, 8, 2 * HEADS), F32),
            pltpu.VMEM((2 * HEADS, LATENT), BF16),
            pltpu.VMEM((8, 2 * HEADS), F32),
            pltpu.VMEM((8, GROUP, LATENT), BF16),
            pltpu.VMEM((8, 8, 2 * HEADS), F32),
            dma((5,)),
            dma,
            dma,
            dma((3,)),
            dma((4,)),
            dma((8,)),
            dma((8,)),
            dma((4,)),
            dma((4,)),
            dma((4,)),
            dma((4,)),
            dma((4,)),
            dma((4,)),
            dma((8,)),
            dma((8,)),
            dma((8,)),
            dma((8,)),
        ],
        compiler_params=pltpu.CompilerParams(
            collective_id=0, has_side_effects=True, vmem_limit_bytes=67_043_328
        ),
    )(
        queries,
        new_latent,
        jnp.swapaxes(cache, 1, 2),
        lengths,
        w_uk.reshape(GROUP * NOPE, LATENT),
        w_uv.reshape(GROUP * LATENT, VDIM),
    )


def solution(mesh):
    return jax.shard_map(
        shards,
        mesh=mesh,
        in_specs=(
            P("seq", "head", None),
            P("seq", None),
            P("head", "seq", None),
            P(),
            P("head", None, None),
            P("head", None, None),
        ),
        out_specs=P("seq", "head", None),
        check_vma=False,
    )
```

```python
import jax
import jax.numpy as jnp
from jax import lax
from jax.experimental import pallas as pl
from jax.experimental.pallas import tpu as pltpu
from jax.sharding import PartitionSpec as P

NOPE = 128
ROPE = 64
LATENT = 512
WIDTH = LATENT + ROPE
VDIM = 128
SPEC = 4
GROUP = 16
HEADS = 64
SLOTS = 128
NEG = -1e30
SCALE = (NOPE + ROPE) ** -0.5
MESH = pl.DeviceIdType.MESH
F32 = jnp.float32
BF16 = jnp.bfloat16


def dot(a, b, dims):
    return lax.dot_general(a, b, (dims, ((), ())), preferred_element_type=F32)


def kernel(
    q_hbm, nl_hbm, cache_hbm, len_ref, wuk_hbm, wuv_hbm, out_ref,
    wuk, wuv, q_in, nl, kt, kv, q_own, q_all, o_out, s_out, o_in, s_in,
    r_out, t_out, r_in, t_in,
    local_sem, swap_send, swap_recv, nl_send, nl_recv, a_send, a_recv, b_send, b_recv,
    o_send, o_recv, s_send, s_recv, r_send, r_recv, t_send, t_recv, ready_a, ready_r,
):
    seq, head = lax.axis_index("seq"), lax.axis_index("head")
    core = lax.rem(seq, 2)
    x = lax.rem(lax.div(seq, 2), 4)
    y = lax.rem(lax.div(seq, 8), 4)
    zhi = lax.div(seq, 32)

    def at(zhi_, y_, x_, core_):
        return ((zhi_ * 4 + y_) * 4 + x_) * 2 + core_

    to_head, to_core = zhi * 2 + lax.div(y, 2), lax.rem(y, 2)
    plane = zhi * 4 + y
    from_zhi, from_y = lax.div(head, 2), lax.rem(head, 2) * 2 + core
    own_piece = (to_head == head) & (to_core == core)
    others_piece = jnp.logical_not(own_piece)

    def worker(j):
        zhi_ = zhi if j < 4 else 1 - zhi
        return at(zhi_, lax.rem(y + j % 4, 4), x, to_core), to_head

    def owner(j):
        return at(from_zhi, from_y, x, lax.rem(core + j // 4, 2)), lax.rem(head + j % 4, 4)

    odd = lax.rem(x, 2)
    near_x, pair_x, upper = x + 1 - 2 * odd, 3 - x, lax.div(x, 2)
    twin = (at(zhi, y, x, 1 - core), head)
    beside = (at(zhi, y, near_x, core), head)
    mates = [twin, beside, (at(zhi, y, near_x, 1 - core), head)]
    pair = [(at(zhi, y, pair_x, core), head), (at(zhi, y, pair_x, 1 - core), head)]

    barrier = pltpu.get_barrier_semaphore()

    def greet(device):
        pl.semaphore_signal(barrier, inc=1, device_id=device, device_id_type=MESH)

    def answer(sem, device):
        pl.semaphore_signal(sem, inc=1, device_id=device, device_id_type=MESH)

    for device in mates + pair:
        greet(device)
    for j in range(1, 4):
        greet(worker(j))

    @pl.when(others_piece)
    def _():
        greet(worker(0))

    @pl.when(zhi == 0)
    def _():
        for j in range(4, 8):
            greet(worker(j))

    @pl.when((zhi == 0) | (from_zhi == zhi))
    def _():
        for j in range(1, 8):
            greet(owner(j))

        @pl.when(others_piece)
        def _():
            greet(owner(0))

    greeted = 9 + 4 * zhi + jnp.where((zhi == 1) | (from_zhi == zhi), 8, 0)
    greeted = greeted - jnp.where(own_piece, 2, 0)

    def remote(src, dst, send, recv, device):
        return pltpu.make_async_remote_copy(
            src_ref=src, dst_ref=dst, send_sem=send, recv_sem=recv,
            device_id=device, device_id_type=MESH,
        )

    def slots(block):
        return kt.at[:, pl.ds(pl.multiple_of(block * SLOTS, SLOTS), SLOTS)]

    token = lax.rem(seq, SPEC)

    load_q = pltpu.make_async_copy(q_hbm.at[0], q_in, local_sem.at[0])
    load_wuk = pltpu.make_async_copy(wuk_hbm, wuk, local_sem.at[1])
    load_nl = pltpu.make_async_copy(nl_hbm, nl.at[token], local_sem.at[2])
    load_kt = pltpu.make_async_copy(
        cache_hbm.at[2 * core + upper], slots(core), local_sem.at[3]
    )
    load_wuv = pltpu.make_async_copy(wuv_hbm, wuv, local_sem.at[4])
    load_q.start()
    load_wuk.start()
    load_nl.start()
    load_kt.start()
    load_wuv.start()

    load_q.wait()
    q = q_in[...]
    row_of = lax.broadcasted_iota(jnp.int32, (GROUP, GROUP * NOPE), 0)
    col_of = lax.broadcasted_iota(jnp.int32, (GROUP, GROUP * NOPE), 1)
    spread = jnp.concatenate([q[:, :NOPE].astype(F32)] * GROUP, axis=1)
    spread = jnp.where(lax.div(col_of, NOPE) == row_of, spread, 0.0).astype(BF16)
    load_wuk.wait()
    absorbed = dot(spread, wuk[...], ((1,), (0,)))
    q_own[:, :LATENT] = absorbed.astype(BF16)
    q_own[:, LATENT:] = q[:, NOPE:]

    pl.semaphore_wait(barrier, greeted)

    my_slot = core * 4 + head

    def rows_of(x_, core_, head_):
        start = pl.multiple_of(GROUP * head_, GROUP)
        return q_all.at[2 * lax.rem(x_, 2) + core_, pl.ds(start, GROUP)]

    my_place = rows_of(x, core, head)

    def send_queries(j):
        return remote(q_own, my_place, a_send.at[j], a_recv.at[my_slot], worker(j))

    for j in range(1, 4):
        send_queries(j).start()

    @pl.when(own_piece)
    def _():
        pltpu.make_async_copy(q_own, my_place, a_recv.at[my_slot]).start()

    @pl.when(others_piece)
    def _():
        send_queries(0).start()

    swaps = [
        remote(cache_hbm.at[2 * (1 - core) + upper], slots(core),
               swap_send.at[0], swap_recv.at[core], twin),
        remote(cache_hbm.at[2 * core + 1 - upper], slots(2 + core),
               swap_send.at[1], swap_recv.at[2 + core], pair[0]),
        remote(cache_hbm.at[2 * (1 - core) + 1 - upper], slots(2 + core),
               swap_send.at[2], swap_recv.at[2 + core], pair[1]),
    ]
    load_nl.wait()
    news = [
        remote(nl.at[token], nl.at[token], nl_send.at[k], nl_recv.at[token], mates[k])
        for k in range(3)
    ]

    @pl.when(zhi == 1)
    def _():
        for j in range(4, 8):
            answer(ready_r, worker(j))

        @pl.when(from_zhi == 0)
        def _():
            for j in range(8):
                answer(ready_a, owner(j))

    for copy in swaps + news:
        copy.start()

    @pl.when(zhi == 0)
    def _():
        pl.semaphore_wait(ready_a, 4)

    for j in range(4, 8):
        send_queries(j).start()

    load_kt.wait()
    for block in (1 - core, 2, 3):
        pltpu.make_async_copy(cache_hbm.at[0], slots(block), swap_recv.at[block]).wait()
    kv[...] = kt[...].T

    def forward(c, g):
        place = rows_of(x, c, g)
        return remote(place, place, b_send.at[4 * c + g], b_recv.at[4 * c + g], beside)

    for g in range(4):
        for c in range(2):
            pltpu.make_async_copy(q_own, rows_of(x, c, g), a_recv.at[4 * c + g]).wait()
            forward(c, g).start()

    chip = lax.div(seq, 2)
    length = len_ref[4 * head + 2 * core + upper]
    step = (3 - 2 * x) * (2 * SLOTS)

    def partial_of(x_):
        queries = q_all[pl.ds(2 * lax.rem(x_, 2), 2)].reshape(2 * HEADS, WIDTH)
        scores = dot(kv[...], queries, ((1,), (1,))) * SCALE
        slot = lax.broadcasted_iota(jnp.int32, scores.shape, 0)
        position = chip * (2 * SLOTS) + jnp.where(
            slot < 2 * SLOTS, slot, slot - 2 * SLOTS + step
        )
        visible = position < length
        top = jnp.max(jnp.where(visible, scores, NEG), axis=0, keepdims=True)
        p = jnp.where(visible, jnp.exp(scores - top), 0.0)
        total = jnp.sum(p, axis=0, keepdims=True)
        weighted = dot(kt[:LATENT], p.astype(BF16), ((1,), (0,)))
        return top, total, weighted

    def put_stats(ref, top, total):
        ref[0:1] = top
        ref[1:2] = total

    top_0, total_0, weighted_0 = partial_of(x)
    for g in range(4):
        for c in range(2):
            pltpu.make_async_copy(q_own, rows_of(near_x, c, g), b_recv.at[4 * c + g]).wait()
    top_1, total_1, weighted_1 = partial_of(near_x)
    o_out[...] = weighted_1.astype(BF16)
    put_stats(s_out, top_1, total_1)
    back = [
        remote(s_out, s_in, s_send, s_recv, beside),
        remote(o_out, o_in, o_send, o_recv, beside),
    ]
    for copy in back:
        copy.start()

    for copy in back:
        copy.wait_recv()
    top_1, total_1 = s_in[0:1], s_in[1:2]
    top = jnp.maximum(top_0, top_1)
    factor_0, factor_1 = jnp.exp(top_0 - top), jnp.exp(top_1 - top)
    put_stats(t_out, top, total_0 * factor_0 + total_1 * factor_1)
    merged = weighted_0 * factor_0 + o_in[...].astype(F32) * factor_1
    r_out[...] = merged.T.astype(BF16)

    def piece(j):
        core_, head_ = lax.rem(core + j // 4, 2), lax.rem(head + j % 4, 4)
        start = pl.multiple_of(HEADS * core_ + GROUP * head_, GROUP)
        return r_out.at[pl.ds(start, GROUP)]

    def send_to_owner(j):
        return (
            remote(t_out, t_in.at[plane], t_send.at[j], t_recv.at[plane], owner(j)),
            remote(piece(j), r_in.at[plane], r_send.at[j], r_recv.at[plane], owner(j)),
        )

    @pl.when((zhi == 0) & (from_zhi == 1))
    def _():
        pl.semaphore_wait(ready_r, 8)

    for j in range(1, 8):
        for copy in send_to_owner(j):
            copy.start()

    @pl.when(own_piece)
    def _():
        pltpu.make_async_copy(t_out, t_in.at[plane], t_recv.at[plane]).start()
        pltpu.make_async_copy(piece(0), r_in.at[plane], r_recv.at[plane]).start()

    @pl.when(others_piece)
    def _():
        for copy in send_to_owner(0):
            copy.start()

    for k in range(1, 4):
        other_token = lax.rem(token + k, SPEC)
        pltpu.make_async_copy(nl.at[token], nl.at[other_token], nl_recv.at[other_token]).wait()
    mine = q_own[...].astype(F32)
    fresh, keys = [], []
    for i in range(SPEC):
        key = nl[i].astype(F32)
        score = jnp.sum(mine * key, axis=1, keepdims=True) * SCALE
        fresh.append(jnp.where(i <= token, score, NEG))
        keys.append(key[:, :LATENT])
    f_top = jnp.maximum(jnp.maximum(fresh[0], fresh[1]), jnp.maximum(fresh[2], fresh[3]))
    f_total, f_weighted = 0.0, 0.0
    for i in range(SPEC):
        p = jnp.where(i <= token, jnp.exp(fresh[i] - f_top), 0.0)
        f_total = f_total + p
        f_weighted = f_weighted + p.astype(BF16).astype(F32) * keys[i]
    load_wuv.wait()

    for k in range(8):
        pltpu.make_async_copy(t_in.at[k], t_in.at[k], t_recv.at[k]).wait()
        pltpu.make_async_copy(r_in.at[k], r_in.at[k], r_recv.at[k]).wait()
    lane = lax.broadcasted_iota(jnp.int32, (GROUP, 2 * HEADS), 1)
    mine_lane = lane == (
        HEADS * core + GROUP * head + lax.broadcasted_iota(jnp.int32, (GROUP, 2 * HEADS), 0)
    )

    def column(row):
        return jnp.sum(jnp.where(mine_lane, row, 0.0), axis=1, keepdims=True)

    tops = [column(t_in[k, 0:1]) for k in range(8)]
    top = f_top
    for t in tops:
        top = jnp.maximum(top, t)
    f_factor = jnp.exp(f_top - top)
    total = f_total * f_factor
    latent = f_weighted * f_factor
    for k in range(8):
        factor = jnp.exp(tops[k] - top)
        total = total + column(t_in[k, 1:2]) * factor
        latent = latent + r_in[k].astype(F32) * factor
    latent = latent / total

    high = latent.astype(BF16).astype(F32)
    both = jnp.concatenate([high, latent - high], axis=0)
    wide = jnp.concatenate([both] * GROUP, axis=1)
    row_of = lax.rem(lax.broadcasted_iota(jnp.int32, wide.shape, 0), GROUP)
    col_of = lax.div(lax.broadcasted_iota(jnp.int32, wide.shape, 1), LATENT)
    wide = jnp.where(row_of == col_of, wide, 0.0).astype(BF16)
    projected = dot(wide, wuv[...], ((1,), (0,)))
    out_ref[0] = (projected[:GROUP] + projected[GROUP:]).astype(BF16)

    for j in range(1, 8):
        send_queries(j).wait_send()
        for copy in send_to_owner(j):
            copy.wait_send()

    @pl.when(others_piece)
    def _():
        send_queries(0).wait_send()
        for copy in send_to_owner(0):
            copy.wait_send()

    for g in range(4):
        for c in range(2):
            forward(c, g).wait_send()
    for copy in swaps + news + back:
        copy.wait_send()


def shards(queries, new_latent, cache, lengths, w_uk, w_uv):
    anywhere = pl.BlockSpec(memory_space=pl.ANY)
    dma = pltpu.SemaphoreType.DMA
    return pl.pallas_call(
        kernel,
        out_shape=jax.ShapeDtypeStruct((1, GROUP, VDIM), BF16),
        in_specs=[
            anywhere,
            anywhere,
            anywhere,
            pl.BlockSpec(memory_space=pltpu.SMEM),
            anywhere,
            anywhere,
        ],
        out_specs=pl.BlockSpec(memory_space=pltpu.VMEM),
        scratch_shapes=[
            pltpu.VMEM((GROUP * NOPE, LATENT), BF16),
            pltpu.VMEM((GROUP * LATENT, VDIM), BF16),
            pltpu.VMEM((GROUP, NOPE + ROPE), BF16),
            pltpu.VMEM((SPEC, 1, WIDTH), BF16),
            pltpu.VMEM((WIDTH, 4 * SLOTS), BF16),
            pltpu.VMEM((4 * SLOTS, WIDTH), BF16),
            pltpu.VMEM((GROUP, WIDTH), BF16),
            pltpu.VMEM((4, HEADS, WIDTH), BF16),
            pltpu.VMEM((LATENT, 2 * HEADS), BF16),
            pltpu.VMEM((2, 2 * HEADS), F32),
            pltpu.VMEM((LATENT, 2 * HEADS), BF16),
            pltpu.VMEM((2, 2 * HEADS), F32),
            pltpu.VMEM((2 * HEADS, LATENT), BF16),
            pltpu.VMEM((2, 2 * HEADS), F32),
            pltpu.VMEM((8, GROUP, LATENT), BF16),
            pltpu.VMEM((8, 2, 2 * HEADS), F32),
            dma((5,)),
            dma((3,)),
            dma((4,)),
            dma((3,)),
            dma((4,)),
            dma((8,)),
            dma((8,)),
            dma((8,)),
            dma((8,)),
            dma,
            dma,
            dma,
            dma,
            dma((8,)),
            dma((8,)),
            dma((8,)),
            dma((8,)),
            pltpu.SemaphoreType.REGULAR,
            pltpu.SemaphoreType.REGULAR,
        ],
        compiler_params=pltpu.CompilerParams(
            collective_id=0, has_side_effects=True, vmem_limit_bytes=67_043_328
        ),
    )(
        queries,
        new_latent,
        jnp.swapaxes(cache, 1, 2),
        lengths,
        w_uk.reshape(GROUP * NOPE, LATENT),
        w_uv.reshape(GROUP * LATENT, VDIM),
    )


def solution(mesh):
    return jax.shard_map(
        shards,
        mesh=mesh,
        in_specs=(
            P("seq", "head", None),
            P("seq", None),
            P("head", "seq", None),
            P(),
            P("head", None, None),
            P("head", None, None),
        ),
        out_specs=P("seq", "head", None),
        check_vma=False,
    )
```

```python
import jax
import jax.numpy as jnp
from jax import lax
from jax.experimental import pallas as pl
from jax.experimental.pallas import tpu as pltpu
from jax.sharding import PartitionSpec as P

NOPE = 128
ROPE = 64
LATENT = 512
WIDTH = LATENT + ROPE
VDIM = 128
SPEC = 4
GROUP = 16
HEADS = 64
SEQS = 16
SLOTS = 128
NEG = -1e30
SCALE = (NOPE + ROPE) ** -0.5
MESH = pl.DeviceIdType.MESH
F32 = jnp.float32
BF16 = jnp.bfloat16


def dot(a, b, dims):
    return lax.dot_general(a, b, (dims, ((), ())), preferred_element_type=F32)


def kernel(
    q_hbm, nl_hbm, cache_hbm, len_hbm, wuk_hbm, wuv_hbm, out_ref,
    len_ref, wuk, wuv, q_in, nl, kt, kv, q_own, q_all, o_out, s_out, o_in, s_in,
    r_out, t_out, r_in, t_in,
    local_sem, swap_send, swap_recv, nl_send, nl_recv, a_send, a_recv, b_send, b_recv,
    o_send, o_recv, s_send, s_recv, r_send, r_recv, t_send, t_recv,
):
    seq, head = lax.axis_index("seq"), lax.axis_index("head")
    core = lax.rem(seq, 2)
    x = lax.rem(lax.div(seq, 2), 4)
    y = lax.rem(lax.div(seq, 8), 4)
    zhi = lax.div(seq, 32)

    def at(zhi_, y_, x_, core_):
        return ((zhi_ * 4 + y_) * 4 + x_) * 2 + core_

    to_head, to_core = zhi * 2 + lax.div(y, 2), lax.rem(y, 2)
    plane = zhi * 4 + y
    from_zhi, from_y = lax.div(head, 2), lax.rem(head, 2) * 2 + core
    own_piece = (to_head == head) & (to_core == core)
    others_piece = jnp.logical_not(own_piece)

    def worker(j):
        zhi_ = zhi if j < 4 else 1 - zhi
        return at(zhi_, lax.rem(y + j % 4, 4), x, to_core), to_head

    def owner(j):
        return at(from_zhi, from_y, x, lax.rem(core + j // 4, 2)), lax.rem(head + j % 4, 4)

    odd = lax.rem(x, 2)
    near_x, pair_x, upper = x + 1 - 2 * odd, 3 - x, lax.div(x, 2)
    twin = (at(zhi, y, x, 1 - core), head)
    beside = (at(zhi, y, near_x, core), head)
    mates = [twin, beside, (at(zhi, y, near_x, 1 - core), head)]
    pair = [(at(zhi, y, pair_x, core), head), (at(zhi, y, pair_x, 1 - core), head)]

    barrier = pltpu.get_barrier_semaphore()

    def greet(device):
        pl.semaphore_signal(barrier, inc=1, device_id=device, device_id_type=MESH)

    for j in range(7, 0, -1):
        greet(worker(j))
        greet(owner(j))

    @pl.when(others_piece)
    def _():
        greet(worker(0))
        greet(owner(0))

    for device in mates + pair:
        greet(device)

    def remote(src, dst, send, recv, device):
        return pltpu.make_async_remote_copy(
            src_ref=src, dst_ref=dst, send_sem=send, recv_sem=recv,
            device_id=device, device_id_type=MESH,
        )

    def slots(block):
        return kt.at[:, pl.ds(pl.multiple_of(block * SLOTS, SLOTS), SLOTS)]

    token = lax.rem(seq, SPEC)

    load_q = pltpu.make_async_copy(q_hbm.at[0], q_in, local_sem.at[0])
    load_wuk = pltpu.make_async_copy(wuk_hbm, wuk, local_sem.at[1])
    load_nl = pltpu.make_async_copy(nl_hbm, nl.at[token], local_sem.at[2])
    load_kt = pltpu.make_async_copy(
        cache_hbm.at[2 * core + upper], slots(core), local_sem.at[3]
    )
    load_wuv = pltpu.make_async_copy(wuv_hbm, wuv, local_sem.at[4])
    load_q.start()
    load_wuk.start()
    load_nl.start()
    load_kt.start()
    load_wuv.start()
    load_len = pltpu.make_async_copy(len_hbm, len_ref, local_sem.at[5])
    load_len.start()

    load_q.wait()
    q = q_in[...]
    row_of = lax.broadcasted_iota(jnp.int32, (GROUP, GROUP * NOPE), 0)
    col_of = lax.broadcasted_iota(jnp.int32, (GROUP, GROUP * NOPE), 1)
    spread = jnp.concatenate([q[:, :NOPE].astype(F32)] * GROUP, axis=1)
    spread = jnp.where(lax.div(col_of, NOPE) == row_of, spread, 0.0).astype(BF16)
    load_wuk.wait()
    absorbed = dot(spread, wuk[...], ((1,), (0,)))
    q_own[:, :LATENT] = absorbed.astype(BF16)
    q_own[:, LATENT:] = q[:, NOPE:]

    pl.semaphore_wait(barrier, jnp.where(own_piece, 19, 21))

    my_slot = core * 4 + head

    def rows_of(x_, core_, head_):
        start = pl.multiple_of(GROUP * head_, GROUP)
        return q_all.at[2 * lax.rem(x_, 2) + core_, pl.ds(start, GROUP)]

    my_place = rows_of(x, core, head)

    def send_queries(j):
        return remote(q_own, my_place, a_send.at[j], a_recv.at[my_slot], worker(j))

    for j in (4, 5, 7, 6, 1, 3, 2):
        send_queries(j).start()

    @pl.when(own_piece)
    def _():
        pltpu.make_async_copy(q_own, my_place, a_recv.at[my_slot]).start()

    @pl.when(others_piece)
    def _():
        send_queries(0).start()

    swaps = [
        remote(cache_hbm.at[2 * (1 - core) + upper], slots(core),
               swap_send.at[0], swap_recv.at[core], twin),
        remote(cache_hbm.at[2 * core + 1 - upper], slots(2 + core),
               swap_send.at[1], swap_recv.at[2 + core], pair[0]),
        remote(cache_hbm.at[2 * (1 - core) + 1 - upper], slots(2 + core),
               swap_send.at[2], swap_recv.at[2 + core], pair[1]),
    ]
    load_nl.wait()
    news = [
        remote(nl.at[token], nl.at[token], nl_send.at[k], nl_recv.at[token], mates[k])
        for k in range(3)
    ]

    for copy in swaps + news:
        copy.start()

    def forward(c, g):
        place = rows_of(x, c, g)
        return remote(place, place, b_send.at[4 * c + g], b_recv.at[4 * c + g], beside)

    for g in range(4):
        for c in range(2):
            pltpu.make_async_copy(q_own, rows_of(x, c, g), a_recv.at[4 * c + g]).wait()
            forward(c, g).start()

    load_kt.wait()
    for block in (1 - core, 2, 3):
        pltpu.make_async_copy(cache_hbm.at[0], slots(block), swap_recv.at[block]).wait()
    kv[...] = kt[...].T

    chip = lax.div(seq, 2)
    load_len.wait()
    length = len_ref[4 * head + 2 * core + upper]
    step = (3 - 2 * x) * (2 * SLOTS)

    def partial_of(x_):
        queries = q_all[pl.ds(2 * lax.rem(x_, 2), 2)].reshape(2 * HEADS, WIDTH)
        scores = dot(kv[...], queries, ((1,), (1,))) * SCALE
        slot = lax.broadcasted_iota(jnp.int32, scores.shape, 0)
        position = chip * (2 * SLOTS) + jnp.where(
            slot < 2 * SLOTS, slot, slot - 2 * SLOTS + step
        )
        visible = position < length
        top = jnp.max(jnp.where(visible, scores, NEG), axis=0, keepdims=True)
        p = jnp.where(visible, jnp.exp(scores - top), 0.0)
        total = jnp.sum(p, axis=0, keepdims=True)
        weighted = dot(kt[:LATENT], p.astype(BF16), ((1,), (0,)))
        return top, total, weighted

    def put_stats(ref, top, total):
        ref[0:1] = top
        ref[1:2] = total

    top_0, total_0, weighted_0 = partial_of(x)
    for g in range(4):
        for c in range(2):
            pltpu.make_async_copy(q_own, rows_of(near_x, c, g), b_recv.at[4 * c + g]).wait()
    top_1, total_1, weighted_1 = partial_of(near_x)
    o_out[...] = weighted_1.astype(BF16)
    put_stats(s_out, top_1, total_1)
    back = [
        remote(s_out, s_in, s_send, s_recv, beside),
        remote(o_out, o_in, o_send, o_recv, beside),
    ]
    for copy in back:
        copy.start()

    for copy in back:
        copy.wait_recv()
    top_1, total_1 = s_in[0:1], s_in[1:2]
    top = jnp.maximum(top_0, top_1)
    factor_0, factor_1 = jnp.exp(top_0 - top), jnp.exp(top_1 - top)
    put_stats(t_out, top, total_0 * factor_0 + total_1 * factor_1)
    merged = weighted_0 * factor_0 + o_in[...].astype(F32) * factor_1
    r_out[...] = merged.T.astype(BF16)

    def piece(j):
        core_, head_ = lax.rem(core + j // 4, 2), lax.rem(head + j % 4, 4)
        start = pl.multiple_of(HEADS * core_ + GROUP * head_, GROUP)
        return r_out.at[pl.ds(start, GROUP)]

    def send_to_owner(j):
        return (
            remote(t_out, t_in.at[plane], t_send.at[j], t_recv.at[plane], owner(j)),
            remote(piece(j), r_in.at[plane], r_send.at[j], r_recv.at[plane], owner(j)),
        )

    for j in range(1, 8):
        for copy in send_to_owner(j):
            copy.start()

    @pl.when(own_piece)
    def _():
        pltpu.make_async_copy(t_out, t_in.at[plane], t_recv.at[plane]).start()
        pltpu.make_async_copy(piece(0), r_in.at[plane], r_recv.at[plane]).start()

    @pl.when(others_piece)
    def _():
        for copy in send_to_owner(0):
            copy.start()

    for k in range(1, 4):
        other_token = lax.rem(token + k, SPEC)
        pltpu.make_async_copy(nl.at[token], nl.at[other_token], nl_recv.at[other_token]).wait()
    mine = q_own[...].astype(F32)
    fresh, keys = [], []
    for i in range(SPEC):
        key = nl[i].astype(F32)
        score = jnp.sum(mine * key, axis=1, keepdims=True) * SCALE
        fresh.append(jnp.where(i <= token, score, NEG))
        keys.append(key[:, :LATENT])
    f_top = jnp.maximum(jnp.maximum(fresh[0], fresh[1]), jnp.maximum(fresh[2], fresh[3]))
    f_total, f_weighted = 0.0, 0.0
    for i in range(SPEC):
        p = jnp.where(i <= token, jnp.exp(fresh[i] - f_top), 0.0)
        f_total = f_total + p
        f_weighted = f_weighted + p.astype(BF16).astype(F32) * keys[i]
    load_wuv.wait()

    for k in range(8):
        pltpu.make_async_copy(t_in.at[k], t_in.at[k], t_recv.at[k]).wait()
        pltpu.make_async_copy(r_in.at[k], r_in.at[k], r_recv.at[k]).wait()
    lane = lax.broadcasted_iota(jnp.int32, (GROUP, 2 * HEADS), 1)
    mine_lane = lane == (
        HEADS * core + GROUP * head + lax.broadcasted_iota(jnp.int32, (GROUP, 2 * HEADS), 0)
    )

    def column(row):
        return jnp.sum(jnp.where(mine_lane, row, 0.0), axis=1, keepdims=True)

    tops = [column(t_in[k, 0:1]) for k in range(8)]
    top = f_top
    for t in tops:
        top = jnp.maximum(top, t)
    f_factor = jnp.exp(f_top - top)
    total = f_total * f_factor
    latent = f_weighted * f_factor
    for k in range(8):
        factor = jnp.exp(tops[k] - top)
        total = total + column(t_in[k, 1:2]) * factor
        latent = latent + r_in[k].astype(F32) * factor
    latent = latent / total

    high = latent.astype(BF16).astype(F32)
    both = jnp.concatenate([high, latent - high], axis=0)
    wide = jnp.concatenate([both] * GROUP, axis=1)
    row_of = lax.rem(lax.broadcasted_iota(jnp.int32, wide.shape, 0), GROUP)
    col_of = lax.div(lax.broadcasted_iota(jnp.int32, wide.shape, 1), LATENT)
    wide = jnp.where(row_of == col_of, wide, 0.0).astype(BF16)
    projected = dot(wide, wuv[...], ((1,), (0,)))
    out_ref[0] = (projected[:GROUP] + projected[GROUP:]).astype(BF16)

    for j in range(1, 8):
        send_queries(j).wait_send()
        for copy in send_to_owner(j):
            copy.wait_send()

    @pl.when(others_piece)
    def _():
        send_queries(0).wait_send()
        for copy in send_to_owner(0):
            copy.wait_send()

    for g in range(4):
        for c in range(2):
            forward(c, g).wait_send()
    for copy in swaps + news + back:
        copy.wait_send()


def shards(queries, new_latent, cache, lengths, w_uk, w_uv):
    anywhere = pl.BlockSpec(memory_space=pltpu.HBM)
    dma = pltpu.SemaphoreType.DMA
    return pl.pallas_call(
        kernel,
        out_shape=jax.ShapeDtypeStruct((1, GROUP, VDIM), BF16),
        in_specs=[
            anywhere,
            anywhere,
            anywhere,
            anywhere,
            anywhere,
            anywhere,
        ],
        out_specs=pl.BlockSpec(memory_space=pltpu.VMEM),
        scratch_shapes=[
            pltpu.SMEM((SEQS,), jnp.int32),
            pltpu.VMEM((GROUP * NOPE, LATENT), BF16),
            pltpu.VMEM((GROUP * LATENT, VDIM), BF16),
            pltpu.VMEM((GROUP, NOPE + ROPE), BF16),
            pltpu.VMEM((SPEC, 1, WIDTH), BF16),
            pltpu.VMEM((WIDTH, 4 * SLOTS), BF16),
            pltpu.VMEM((4 * SLOTS, WIDTH), BF16),
            pltpu.VMEM((GROUP, WIDTH), BF16),
            pltpu.VMEM((4, HEADS, WIDTH), BF16),
            pltpu.VMEM((LATENT, 2 * HEADS), BF16),
            pltpu.VMEM((2, 2 * HEADS), F32),
            pltpu.VMEM((LATENT, 2 * HEADS), BF16),
            pltpu.VMEM((2, 2 * HEADS), F32),
            pltpu.VMEM((2 * HEADS, LATENT), BF16),
            pltpu.VMEM((2, 2 * HEADS), F32),
            pltpu.VMEM((8, GROUP, LATENT), BF16),
            pltpu.VMEM((8, 2, 2 * HEADS), F32),
            dma((6,)),
            dma((3,)),
            dma((4,)),
            dma((3,)),
            dma((4,)),
            dma((8,)),
            dma((8,)),
            dma((8,)),
            dma((8,)),
            dma,
            dma,
            dma,
            dma,
            dma((8,)),
            dma((8,)),
            dma((8,)),
            dma((8,)),
        ],
        compiler_params=pltpu.CompilerParams(
            collective_id=0, has_side_effects=True, vmem_limit_bytes=40 << 20
        ),
    )(*[
        pltpu.with_memory_space_constraint(array, pltpu.HBM)
        for array in (
            queries,
            new_latent,
            jnp.swapaxes(cache, 1, 2),
            lengths,
            w_uk.reshape(GROUP * NOPE, LATENT),
            w_uv.reshape(GROUP * LATENT, VDIM),
        )
    ])


def solution(mesh):
    return jax.shard_map(
        shards,
        mesh=mesh,
        in_specs=(
            P("seq", "head", None),
            P("seq", None),
            P("head", "seq", None),
            P(),
            P("head", None, None),
            P("head", None, None),
        ),
        out_specs=P("seq", "head", None),
        check_vma=False,
    )
```

```python
import jax
import jax.numpy as jnp
from jax import lax
from jax.experimental import pallas as pl
from jax.experimental.pallas import tpu as pltpu
from jax.sharding import PartitionSpec as P

NOPE = 128
ROPE = 64
LATENT = 512
WIDTH = LATENT + ROPE
VDIM = 128
SPEC = 4
GROUP = 16
HEADS = 64
SEQS = 16
SLOTS = 128
NEG = -1e30
PACKED = GROUP * WIDTH // 128
SCALE = (NOPE + ROPE) ** -0.5
MESH = pl.DeviceIdType.MESH
F32 = jnp.float32
BF16 = jnp.bfloat16


def dot(a, b, dims):
    return lax.dot_general(a, b, (dims, ((), ())), preferred_element_type=F32)


def kernel(
    q_hbm, nl_hbm, cache_hbm, len_hbm, wuk_hbm, wuv_hbm, out_ref,
    len_ref, wuk, wuv, q_in, nl, kt, kv, q_own, q_all, o_out, s_out, o_in, s_in,
    r_out, t_out, r_in, t_in,
    local_sem, swap_send, swap_recv, nl_send, nl_recv, a_send, a_recv, f_send, b_send, b_recv,
    o_send, o_recv, s_send, s_recv, r_send, r_recv, t_send, t_recv,
):
    seq, head = lax.axis_index("seq"), lax.axis_index("head")
    core = lax.rem(seq, 2)
    x = lax.rem(lax.div(seq, 2), 4)
    y = lax.rem(lax.div(seq, 8), 4)
    zhi = lax.div(seq, 32)

    def at(zhi_, y_, x_, core_):
        return ((zhi_ * 4 + y_) * 4 + x_) * 2 + core_

    to_head, to_core = zhi * 2 + lax.div(y, 2), lax.rem(y, 2)
    plane = zhi * 4 + y
    from_zhi, from_y = lax.div(head, 2), lax.rem(head, 2) * 2 + core
    own_piece = (to_head == head) & (to_core == core)
    others_piece = jnp.logical_not(own_piece)

    def worker(j):
        zhi_ = zhi if j < 4 else 1 - zhi
        return at(zhi_, lax.rem(y + j % 4, 4), x, to_core), to_head

    def owner(j):
        return at(from_zhi, from_y, x, lax.rem(core + j // 4, 2)), lax.rem(head + j % 4, 4)

    odd = lax.rem(x, 2)
    relays = (from_zhi != zhi) & (from_y == y)
    along_y = [(at(zhi, lax.rem(y + d, 4), x, core), head) for d in (1, 3, 2)]
    near_x, pair_x, upper = x + 1 - 2 * odd, 3 - x, lax.div(x, 2)
    twin = (at(zhi, y, x, 1 - core), head)
    beside = (at(zhi, y, near_x, core), head)
    mates = [twin, beside, (at(zhi, y, near_x, 1 - core), head)]
    pair = [(at(zhi, y, pair_x, core), head), (at(zhi, y, pair_x, 1 - core), head)]

    barrier = pltpu.get_barrier_semaphore()

    def greet(device):
        pl.semaphore_signal(barrier, inc=1, device_id=device, device_id_type=MESH)

    for j in range(7, 0, -1):
        greet(worker(j))
        greet(owner(j))

    @pl.when(others_piece)
    def _():
        greet(worker(0))
        greet(owner(0))

    for device in mates + pair + along_y:
        greet(device)

    def remote(src, dst, send, recv, device):
        return pltpu.make_async_remote_copy(
            src_ref=src, dst_ref=dst, send_sem=send, recv_sem=recv,
            device_id=device, device_id_type=MESH,
        )

    def slots(block):
        return kt.at[:, pl.ds(pl.multiple_of(block * SLOTS, SLOTS), SLOTS)]

    token = lax.rem(seq, SPEC)

    load_q = pltpu.make_async_copy(q_hbm.at[0], q_in, local_sem.at[0])
    load_wuk = pltpu.make_async_copy(wuk_hbm, wuk, local_sem.at[1])
    load_nl = pltpu.make_async_copy(nl_hbm, nl.at[token], local_sem.at[2])
    load_kt = pltpu.make_async_copy(
        cache_hbm.at[2 * core + upper], slots(core), local_sem.at[3]
    )
    load_wuv = pltpu.make_async_copy(wuv_hbm, wuv, local_sem.at[4])
    load_q.start()
    load_wuk.start()
    load_nl.start()
    load_kt.start()
    load_wuv.start()
    load_len = pltpu.make_async_copy(len_hbm, len_ref, local_sem.at[5])
    load_len.start()

    load_q.wait()
    q = q_in[...]
    row_of = lax.broadcasted_iota(jnp.int32, (GROUP, GROUP * NOPE), 0)
    col_of = lax.broadcasted_iota(jnp.int32, (GROUP, GROUP * NOPE), 1)
    diagonal = jnp.concatenate([q[:, :NOPE].astype(F32)] * GROUP, axis=1)
    diagonal = jnp.where(lax.div(col_of, NOPE) == row_of, diagonal, 0.0).astype(BF16)
    load_wuk.wait()
    absorbed = dot(diagonal, wuk[...], ((1,), (0,)))
    for i in range(4):
        q_own[GROUP * i : GROUP * (i + 1)] = absorbed[:, 128 * i : 128 * (i + 1)].astype(BF16)
    rope = q[:, NOPE:].astype(F32)
    rope = jnp.concatenate([rope[: GROUP // 2], rope[GROUP // 2 :]], axis=1)
    q_own[4 * GROUP :] = rope.astype(BF16)

    pl.semaphore_wait(barrier, jnp.where(own_piece, 22, 24))

    my_slot = core * 4 + head

    def rows_of(x_, core_, head_):
        return q_all.at[2 * lax.rem(x_, 2) + core_, head_]

    my_place = rows_of(x, core, head)

    def send_queries(j):
        return remote(q_own, my_place, a_send.at[j], a_recv.at[my_slot], worker(j))

    for j in (4, 1, 3, 2):
        send_queries(j).start()

    @pl.when(own_piece)
    def _():
        pltpu.make_async_copy(q_own, my_place, a_recv.at[my_slot]).start()

    @pl.when(others_piece)
    def _():
        send_queries(0).start()

    swaps = [
        remote(cache_hbm.at[2 * (1 - core) + upper], slots(core),
               swap_send.at[0], swap_recv.at[core], twin),
        remote(cache_hbm.at[2 * core + 1 - upper], slots(2 + core),
               swap_send.at[1], swap_recv.at[2 + core], pair[0]),
        remote(cache_hbm.at[2 * (1 - core) + 1 - upper], slots(2 + core),
               swap_send.at[2], swap_recv.at[2 + core], pair[1]),
    ]
    load_nl.wait()
    news = [
        remote(nl.at[token], nl.at[token], nl_send.at[k], nl_recv.at[token], mates[k])
        for k in range(3)
    ]

    for copy in swaps + news:
        copy.start()

    def forward(c, g):
        place = rows_of(x, c, g)
        return remote(place, place, b_send.at[4 * c + g], b_recv.at[4 * c + g], beside)

    def spread(c, g):
        place = rows_of(x, c, g)
        return [
            remote(place, place, f_send.at[d, 4 * c + g], a_recv.at[4 * c + g], along_y[d])
            for d in range(3)
        ]

    for k in range(4):
        g = jnp.where(zhi == 0, k, 3 - k)
        for c in range(2):
            pltpu.make_async_copy(q_own, rows_of(x, c, g), a_recv.at[4 * c + g]).wait()

            @pl.when(relays)
            def _():
                for copy in spread(c, g):
                    copy.start()

            forward(c, g).start()

    load_kt.wait()
    for block in (1 - core, 2, 3):
        pltpu.make_async_copy(cache_hbm.at[0], slots(block), swap_recv.at[block]).wait()
    kv[:, :LATENT] = kt[:LATENT].T
    kv[:, LATENT:] = jnp.concatenate([kt[LATENT:], kt[LATENT:]], axis=0).T

    chip = lax.div(seq, 2)
    load_len.wait()
    length = len_ref[4 * head + 2 * core + upper]
    step = (3 - 2 * x) * (2 * SLOTS)

    def partial_of(x_):
        pieces = pl.ds(2 * lax.rem(x_, 2), 2)
        queries = [
            q_all[pieces, :, GROUP * i : GROUP * (i + 1)].reshape(2 * HEADS, 128)
            for i in range(4)
        ]
        ropes = q_all[pieces, :, 4 * GROUP :].astype(F32)
        first = lax.broadcasted_iota(jnp.int32, ropes.shape, 3) < ROPE
        ropes = jnp.concatenate(
            [jnp.where(first, ropes, 0.0), jnp.where(first, 0.0, ropes)], axis=2
        )
        queries.append(ropes.reshape(2 * HEADS, 128).astype(BF16))
        queries = jnp.concatenate(queries, axis=1)
        scores = dot(kv[...], queries, ((1,), (1,))) * SCALE
        slot = lax.broadcasted_iota(jnp.int32, scores.shape, 0)
        position = chip * (2 * SLOTS) + jnp.where(
            slot < 2 * SLOTS, slot, slot - 2 * SLOTS + step
        )
        visible = position < length
        top = jnp.max(jnp.where(visible, scores, NEG), axis=0, keepdims=True)
        p = jnp.where(visible, jnp.exp(scores - top), 0.0)
        total = jnp.sum(p, axis=0, keepdims=True)
        weighted = dot(kt[:LATENT], p.astype(BF16), ((1,), (0,)))
        return top, total, weighted

    def put_stats(ref, top, total):
        ref[0:1] = top
        ref[1:2] = total

    top_0, total_0, weighted_0 = partial_of(x)
    for g in range(4):
        for c in range(2):
            pltpu.make_async_copy(q_own, rows_of(near_x, c, g), b_recv.at[4 * c + g]).wait()
    top_1, total_1, weighted_1 = partial_of(near_x)
    o_out[...] = weighted_1.astype(BF16)
    put_stats(s_out, top_1, total_1)
    back = [
        remote(s_out, s_in, s_send, s_recv, beside),
        remote(o_out, o_in, o_send, o_recv, beside),
    ]
    for copy in back:
        copy.start()

    for copy in back:
        copy.wait_recv()
    top_1, total_1 = s_in[0:1], s_in[1:2]
    top = jnp.maximum(top_0, top_1)
    factor_0, factor_1 = jnp.exp(top_0 - top), jnp.exp(top_1 - top)
    put_stats(t_out, top, total_0 * factor_0 + total_1 * factor_1)
    merged = weighted_0 * factor_0 + o_in[...].astype(F32) * factor_1
    r_out[...] = merged.T.astype(BF16)

    def piece(j):
        core_, head_ = lax.rem(core + j // 4, 2), lax.rem(head + j % 4, 4)
        start = pl.multiple_of(HEADS * core_ + GROUP * head_, GROUP)
        return r_out.at[pl.ds(start, GROUP)]

    def send_to_owner(j):
        return (
            remote(t_out, t_in.at[plane], t_send.at[j], t_recv.at[plane], owner(j)),
            remote(piece(j), r_in.at[plane], r_send.at[j], r_recv.at[plane], owner(j)),
        )

    for j in range(1, 8):
        for copy in send_to_owner(j):
            copy.start()

    @pl.when(own_piece)
    def _():
        pltpu.make_async_copy(t_out, t_in.at[plane], t_recv.at[plane]).start()
        pltpu.make_async_copy(piece(0), r_in.at[plane], r_recv.at[plane]).start()

    @pl.when(others_piece)
    def _():
        for copy in send_to_owner(0):
            copy.start()

    for k in range(1, 4):
        other_token = lax.rem(token + k, SPEC)
        pltpu.make_async_copy(nl.at[token], nl.at[other_token], nl_recv.at[other_token]).wait()
    mine = [q_own[GROUP * i : GROUP * (i + 1)].astype(F32) for i in range(4)]
    mine = jnp.concatenate(mine + [q_in[:, NOPE:].astype(F32)], axis=1)
    fresh, keys = [], []
    for i in range(SPEC):
        key = nl[i].astype(F32)
        score = jnp.sum(mine * key, axis=1, keepdims=True) * SCALE
        fresh.append(jnp.where(i <= token, score, NEG))
        keys.append(key[:, :LATENT])
    f_top = jnp.maximum(jnp.maximum(fresh[0], fresh[1]), jnp.maximum(fresh[2], fresh[3]))
    f_total, f_weighted = 0.0, 0.0
    for i in range(SPEC):
        p = jnp.where(i <= token, jnp.exp(fresh[i] - f_top), 0.0)
        f_total = f_total + p
        f_weighted = f_weighted + p.astype(BF16).astype(F32) * keys[i]
    load_wuv.wait()

    for k in range(8):
        pltpu.make_async_copy(t_in.at[k], t_in.at[k], t_recv.at[k]).wait()
        pltpu.make_async_copy(r_in.at[k], r_in.at[k], r_recv.at[k]).wait()
    lane = lax.broadcasted_iota(jnp.int32, (GROUP, 2 * HEADS), 1)
    mine_lane = lane == (
        HEADS * core + GROUP * head + lax.broadcasted_iota(jnp.int32, (GROUP, 2 * HEADS), 0)
    )

    def column(row):
        return jnp.sum(jnp.where(mine_lane, row, 0.0), axis=1, keepdims=True)

    tops = [column(t_in[k, 0:1]) for k in range(8)]
    top = f_top
    for t in tops:
        top = jnp.maximum(top, t)
    f_factor = jnp.exp(f_top - top)
    total = f_total * f_factor
    latent = f_weighted * f_factor
    for k in range(8):
        factor = jnp.exp(tops[k] - top)
        total = total + column(t_in[k, 1:2]) * factor
        latent = latent + r_in[k].astype(F32) * factor
    latent = latent / total

    high = latent.astype(BF16).astype(F32)
    both = jnp.concatenate([high, latent - high], axis=0)
    wide = jnp.concatenate([both] * GROUP, axis=1)
    row_of = lax.rem(lax.broadcasted_iota(jnp.int32, wide.shape, 0), GROUP)
    col_of = lax.div(lax.broadcasted_iota(jnp.int32, wide.shape, 1), LATENT)
    wide = jnp.where(row_of == col_of, wide, 0.0).astype(BF16)
    projected = dot(wide, wuv[...], ((1,), (0,)))
    out_ref[0] = (projected[:GROUP] + projected[GROUP:]).astype(BF16)

    for j in range(1, 8):
        for copy in send_to_owner(j):
            copy.wait_send()
    for j in range(1, 5):
        send_queries(j).wait_send()

    @pl.when(others_piece)
    def _():
        send_queries(0).wait_send()
        for copy in send_to_owner(0):
            copy.wait_send()

    for g in range(4):
        for c in range(2):
            forward(c, g).wait_send()

    @pl.when(relays)
    def _():
        for g in range(4):
            for c in range(2):
                for copy in spread(c, g):
                    copy.wait_send()

    for copy in swaps + news + back:
        copy.wait_send()


def shards(queries, new_latent, cache, lengths, w_uk, w_uv):
    anywhere = pl.BlockSpec(memory_space=pltpu.HBM)
    dma = pltpu.SemaphoreType.DMA
    return pl.pallas_call(
        kernel,
        out_shape=jax.ShapeDtypeStruct((1, GROUP, VDIM), BF16),
        in_specs=[
            anywhere,
            anywhere,
            anywhere,
            anywhere,
            anywhere,
            anywhere,
        ],
        out_specs=pl.BlockSpec(memory_space=pltpu.VMEM),
        scratch_shapes=[
            pltpu.SMEM((SEQS,), jnp.int32),
            pltpu.VMEM((GROUP * NOPE, LATENT), BF16),
            pltpu.VMEM((GROUP * LATENT, VDIM), BF16),
            pltpu.VMEM((GROUP, NOPE + ROPE), BF16),
            pltpu.VMEM((SPEC, 1, WIDTH), BF16),
            pltpu.VMEM((WIDTH, 4 * SLOTS), BF16),
            pltpu.VMEM((4 * SLOTS, LATENT + 128), BF16),
            pltpu.VMEM((PACKED, 128), BF16),
            pltpu.VMEM((4, 4, PACKED, 128), BF16),
            pltpu.VMEM((LATENT, 2 * HEADS), BF16),
            pltpu.VMEM((2, 2 * HEADS), F32),
            pltpu.VMEM((LATENT, 2 * HEADS), BF16),
            pltpu.VMEM((2, 2 * HEADS), F32),
            pltpu.VMEM((2 * HEADS, LATENT), BF16),
            pltpu.VMEM((2, 2 * HEADS), F32),
            pltpu.VMEM((8, GROUP, LATENT), BF16),
            pltpu.VMEM((8, 2, 2 * HEADS), F32),
            dma((6,)),
            dma((3,)),
            dma((4,)),
            dma((3,)),
            dma((4,)),
            dma((8,)),
            dma((8,)),
            dma((3, 8)),
            dma((8,)),
            dma((8,)),
            dma,
            dma,
            dma,
            dma,
            dma((8,)),
            dma((8,)),
            dma((8,)),
            dma((8,)),
        ],
        compiler_params=pltpu.CompilerParams(
            collective_id=0, has_side_effects=True, vmem_limit_bytes=40 << 20
        ),
    )(*[
        pltpu.with_memory_space_constraint(array, pltpu.HBM)
        for array in (
            queries,
            new_latent,
            jnp.swapaxes(cache, 1, 2),
            lengths,
            w_uk.reshape(GROUP * NOPE, LATENT),
            w_uv.reshape(GROUP * LATENT, VDIM),
        )
    ])


def solution(mesh):
    return jax.shard_map(
        shards,
        mesh=mesh,
        in_specs=(
            P("seq", "head", None),
            P("seq", None),
            P("head", "seq", None),
            P(),
            P("head", None, None),
            P("head", None, None),
        ),
        out_specs=P("seq", "head", None),
        check_vma=False,
    )
```

```python
import jax
import jax.numpy as jnp
from jax import lax
from jax.experimental import pallas as pl
from jax.experimental.pallas import tpu as pltpu
from jax.sharding import PartitionSpec as P

NOPE = 128
ROPE = 64
LATENT = 512
WIDTH = LATENT + ROPE
VDIM = 128
SPEC = 4
GROUP = 16
HEADS = 64
PARTS = 2
PART = LATENT // PARTS
SEQS = 16
SLOTS = 128
NEG = -1e30
PACKED = GROUP * WIDTH // 128
SCALE = (NOPE + ROPE) ** -0.5
MESH = pl.DeviceIdType.MESH
F32 = jnp.float32
BF16 = jnp.bfloat16


def dot(a, b, dims):
    return lax.dot_general(a, b, (dims, ((), ())), preferred_element_type=F32)


def kernel(
    q_hbm, nl_hbm, cache_hbm, len_hbm, wuk_hbm, wuv_hbm, out_ref,
    len_ref, wuk, wuv, q_in, nl, kt, kv, q_own, q_all, o_out, s_out, o_in, s_in,
    r_out, t_out, r_in, t_in,
    local_sem, swap_send, swap_recv, nl_send, nl_recv, a_send, a_recv, f_send, b_send, b_recv,
    o_send, o_recv, s_send, s_recv, r_send, r_recv, t_send, t_recv,
):
    seq, head = lax.axis_index("seq"), lax.axis_index("head")
    core = lax.rem(seq, 2)
    x = lax.rem(lax.div(seq, 2), 4)
    y = lax.rem(lax.div(seq, 8), 4)
    zhi = lax.div(seq, 32)

    def at(zhi_, y_, x_, core_):
        return ((zhi_ * 4 + y_) * 4 + x_) * 2 + core_

    to_head, to_core = zhi * 2 + lax.div(y, 2), lax.rem(y, 2)
    plane = zhi * 4 + y
    from_zhi, from_y = lax.div(head, 2), lax.rem(head, 2) * 2 + core
    own_piece = (to_head == head) & (to_core == core)
    others_piece = jnp.logical_not(own_piece)

    def worker(j):
        zhi_ = zhi if j < 4 else 1 - zhi
        return at(zhi_, lax.rem(y + j % 4, 4), x, to_core), to_head

    def owner(j):
        return at(from_zhi, from_y, x, lax.rem(core + j // 4, 2)), lax.rem(head + j % 4, 4)

    odd = lax.rem(x, 2)
    y_from = lax.rem(y + 4 - from_y, 4)
    relays = (from_zhi != zhi) & (y_from == 0)
    passes = (from_zhi != zhi) & (y_from == 3 - 2 * core)
    along_y = [(at(zhi, lax.rem(y + d, 4), x, core), head) for d in (1, 3)]
    onward_y = (at(zhi, lax.rem(y + 3 - 2 * core, 4), x, core), head)
    near_x, pair_x, upper = x + 1 - 2 * odd, 3 - x, lax.div(x, 2)
    twin = (at(zhi, y, x, 1 - core), head)
    beside = (at(zhi, y, near_x, core), head)
    mates = [twin, beside, (at(zhi, y, near_x, 1 - core), head)]
    pair = [(at(zhi, y, pair_x, core), head), (at(zhi, y, pair_x, 1 - core), head)]

    barrier = pltpu.get_barrier_semaphore()

    def greet(device):
        pl.semaphore_signal(barrier, inc=1, device_id=device, device_id_type=MESH)

    @pl.when((from_zhi == zhi) | (from_y == y))
    def _():
        for j in range(7, 0, -1):
            greet(owner(j))

        @pl.when(others_piece)
        def _():
            greet(owner(0))

    for device in mates + pair + along_y:
        greet(device)

    def remote(src, dst, send, recv, device):
        return pltpu.make_async_remote_copy(
            src_ref=src, dst_ref=dst, send_sem=send, recv_sem=recv,
            device_id=device, device_id_type=MESH,
        )

    def slots(block):
        return kt.at[:, pl.ds(pl.multiple_of(block * SLOTS, SLOTS), SLOTS)]

    token = lax.rem(seq, SPEC)

    load_q = pltpu.make_async_copy(q_hbm.at[0], q_in, local_sem.at[0])
    load_wuk = pltpu.make_async_copy(wuk_hbm, wuk, local_sem.at[1])
    load_nl = pltpu.make_async_copy(nl_hbm, nl.at[token], local_sem.at[2])
    load_kt = pltpu.make_async_copy(
        cache_hbm.at[2 * core + upper], slots(core), local_sem.at[3]
    )
    load_wuv = pltpu.make_async_copy(wuv_hbm, wuv, local_sem.at[4])
    load_q.start()
    load_wuk.start()
    load_nl.start()
    load_kt.start()
    load_wuv.start()
    load_len = pltpu.make_async_copy(len_hbm, len_ref, local_sem.at[5])
    load_len.start()

    load_q.wait()
    q = q_in[...]
    row_of = lax.broadcasted_iota(jnp.int32, (GROUP, GROUP * NOPE), 0)
    col_of = lax.broadcasted_iota(jnp.int32, (GROUP, GROUP * NOPE), 1)
    diagonal = jnp.concatenate([q[:, :NOPE].astype(F32)] * GROUP, axis=1)
    diagonal = jnp.where(lax.div(col_of, NOPE) == row_of, diagonal, 0.0).astype(BF16)
    load_wuk.wait()
    absorbed = dot(diagonal, wuk[...], ((1,), (0,)))
    for i in range(4):
        q_own[GROUP * i : GROUP * (i + 1)] = absorbed[:, 128 * i : 128 * (i + 1)].astype(BF16)
    rope = q[:, NOPE:].astype(F32)
    rope = jnp.concatenate([rope[: GROUP // 2], rope[GROUP // 2 :]], axis=1)
    q_own[4 * GROUP :] = rope.astype(BF16)

    pl.semaphore_wait(barrier, jnp.where(own_piece, 11, 12))

    my_slot = core * 4 + head

    def rows_of(x_, core_, head_):
        return q_all.at[2 * lax.rem(x_, 2) + core_, head_]

    my_place = rows_of(x, core, head)

    def send_queries(j):
        return remote(q_own, my_place, a_send.at[j], a_recv.at[my_slot], worker(j))

    for j in (4, 1, 3, 2):
        send_queries(j).start()

    @pl.when(own_piece)
    def _():
        pltpu.make_async_copy(q_own, my_place, a_recv.at[my_slot]).start()

    @pl.when(others_piece)
    def _():
        send_queries(0).start()

    swaps = [
        remote(cache_hbm.at[2 * (1 - core) + upper], slots(core),
               swap_send.at[0], swap_recv.at[core], twin),
        remote(cache_hbm.at[2 * core + 1 - upper], slots(2 + core),
               swap_send.at[1], swap_recv.at[2 + core], pair[0]),
        remote(cache_hbm.at[2 * (1 - core) + 1 - upper], slots(2 + core),
               swap_send.at[2], swap_recv.at[2 + core], pair[1]),
    ]
    load_nl.wait()
    news = [
        remote(nl.at[token], nl.at[token], nl_send.at[k], nl_recv.at[token], mates[k])
        for k in range(3)
    ]

    for copy in swaps + news:
        copy.start()

    def forward(c, g):
        place = rows_of(x, c, g)
        return remote(place, place, b_send.at[4 * c + g], b_recv.at[4 * c + g], beside)

    def spread(c, g):
        place = rows_of(x, c, g)
        return [
            remote(place, place, f_send.at[d, 4 * c + g], a_recv.at[4 * c + g], along_y[d])
            for d in range(2)
        ]

    def pass_on(c, g):
        place = rows_of(x, c, g)
        return remote(
            place, place, f_send.at[0, 4 * c + g], a_recv.at[4 * c + g], onward_y
        )

    for k in range(4):
        g = jnp.where(zhi == 0, k, 3 - k)
        for c in range(2):
            pltpu.make_async_copy(q_own, rows_of(x, c, g), a_recv.at[4 * c + g]).wait()

            @pl.when(relays)
            def _():
                for copy in spread(c, g):
                    copy.start()

            @pl.when(passes)
            def _():
                pass_on(c, g).start()

            forward(c, g).start()

    load_kt.wait()
    for block in (1 - core, 2, 3):
        pltpu.make_async_copy(cache_hbm.at[0], slots(block), swap_recv.at[block]).wait()
    kv[:, :LATENT] = kt[:LATENT].T
    kv[:, LATENT:] = jnp.concatenate([kt[LATENT:], kt[LATENT:]], axis=0).T

    chip = lax.div(seq, 2)
    load_len.wait()
    length = len_ref[4 * head + 2 * core + upper]
    step = (3 - 2 * x) * (2 * SLOTS)

    def partial_of(x_):
        pieces = pl.ds(2 * lax.rem(x_, 2), 2)
        queries = [
            q_all[pieces, :, GROUP * i : GROUP * (i + 1)].reshape(2 * HEADS, 128)
            for i in range(4)
        ]
        ropes = q_all[pieces, :, 4 * GROUP :].astype(F32)
        first = lax.broadcasted_iota(jnp.int32, ropes.shape, 3) < ROPE
        ropes = jnp.concatenate(
            [jnp.where(first, ropes, 0.0), jnp.where(first, 0.0, ropes)], axis=2
        )
        queries.append(ropes.reshape(2 * HEADS, 128).astype(BF16))
        queries = jnp.concatenate(queries, axis=1)
        scores = dot(kv[...], queries, ((1,), (1,))) * SCALE
        slot = lax.broadcasted_iota(jnp.int32, scores.shape, 0)
        position = chip * (2 * SLOTS) + jnp.where(
            slot < 2 * SLOTS, slot, slot - 2 * SLOTS + step
        )
        visible = position < length
        top = jnp.max(jnp.where(visible, scores, NEG), axis=0, keepdims=True)
        p = jnp.where(visible, jnp.exp(scores - top), 0.0)
        total = jnp.sum(p, axis=0, keepdims=True)
        return top, total, p.astype(BF16)

    def weighted_of(p, j):
        return dot(kt[PART * j : PART * (j + 1)], p, ((1,), (0,)))

    def put_stats(ref, top, total):
        ref[0:1] = top
        ref[1:2] = total

    for k in range(4):
        for c in range(2):
            pltpu.make_async_copy(q_own, rows_of(near_x, c, k), b_recv.at[4 * c + k]).wait()
    top_1, total_1, p_1 = partial_of(near_x)
    put_stats(s_out, top_1, total_1)
    back_s = remote(s_out, s_in, s_send, s_recv, beside)
    back_s.start()
    back = []
    for j in range(PARTS):
        o_out[j] = weighted_of(p_1, j).astype(BF16)
        back.append(remote(o_out.at[j], o_in.at[j], o_send.at[j], o_recv.at[j], beside))
        back[j].start()
    top_0, total_0, p_0 = partial_of(x)
    weighted_0 = [weighted_of(p_0, j) for j in range(PARTS)]

    back_s.wait_recv()
    top_1, total_1 = s_in[0:1], s_in[1:2]
    top = jnp.maximum(top_0, top_1)
    factor_0, factor_1 = jnp.exp(top_0 - top), jnp.exp(top_1 - top)
    put_stats(t_out, top, total_0 * factor_0 + total_1 * factor_1)

    def place_of(j):
        core_, head_ = lax.rem(core + j // 4, 2), lax.rem(head + j % 4, 4)
        return pl.ds(pl.multiple_of(HEADS * core_ + GROUP * head_, GROUP), GROUP)

    def send_stats(j):
        return remote(t_out, t_in.at[plane], t_send.at[j], t_recv.at[plane], owner(j))

    def send_part(j, i):
        return remote(
            r_out.at[i, place_of(j)], r_in.at[plane, i], r_send.at[j, i],
            r_recv.at[plane, i], owner(j),
        )

    def to_owners(send, keep):
        for j in range(7, 0, -1):
            send(j).start()

        @pl.when(own_piece)
        def _():
            keep().start()

        @pl.when(others_piece)
        def _():
            send(0).start()

    to_owners(
        send_stats,
        lambda: pltpu.make_async_copy(t_out, t_in.at[plane], t_recv.at[plane]),
    )
    for i in range(PARTS):
        back[i].wait_recv()
        merged = weighted_0[i] * factor_0 + o_in[i].astype(F32) * factor_1
        r_out[i] = merged.T.astype(BF16)
        to_owners(
            lambda j, i=i: send_part(j, i),
            lambda i=i: pltpu.make_async_copy(
                r_out.at[i, place_of(0)], r_in.at[plane, i], r_recv.at[plane, i]
            ),
        )

    for k in range(1, 4):
        other_token = lax.rem(token + k, SPEC)
        pltpu.make_async_copy(nl.at[token], nl.at[other_token], nl_recv.at[other_token]).wait()
    mine = [q_own[GROUP * i : GROUP * (i + 1)].astype(F32) for i in range(4)]
    mine = jnp.concatenate(mine + [q_in[:, NOPE:].astype(F32)], axis=1)
    fresh, keys = [], []
    for i in range(SPEC):
        key = nl[i].astype(F32)
        score = jnp.sum(mine * key, axis=1, keepdims=True) * SCALE
        fresh.append(jnp.where(i <= token, score, NEG))
        keys.append(key[:, :LATENT])
    f_top = jnp.maximum(jnp.maximum(fresh[0], fresh[1]), jnp.maximum(fresh[2], fresh[3]))
    f_total, f_weighted = 0.0, 0.0
    for i in range(SPEC):
        p = jnp.where(i <= token, jnp.exp(fresh[i] - f_top), 0.0)
        f_total = f_total + p
        f_weighted = f_weighted + p.astype(BF16).astype(F32) * keys[i]
    load_wuv.wait()

    for k in range(8):
        pltpu.make_async_copy(t_in.at[k], t_in.at[k], t_recv.at[k]).wait()
        for i in range(PARTS):
            pltpu.make_async_copy(r_in.at[k, i], r_in.at[k, i], r_recv.at[k, i]).wait()
    lane = lax.broadcasted_iota(jnp.int32, (GROUP, 2 * HEADS), 1)
    mine_lane = lane == (
        HEADS * core + GROUP * head + lax.broadcasted_iota(jnp.int32, (GROUP, 2 * HEADS), 0)
    )

    def column(row):
        return jnp.sum(jnp.where(mine_lane, row, 0.0), axis=1, keepdims=True)

    tops = [column(t_in[k, 0:1]) for k in range(8)]
    top = f_top
    for t in tops:
        top = jnp.maximum(top, t)
    f_factor = jnp.exp(f_top - top)
    total = f_total * f_factor
    latent = f_weighted * f_factor
    for k in range(8):
        factor = jnp.exp(tops[k] - top)
        total = total + column(t_in[k, 1:2]) * factor
        parts = jnp.concatenate([r_in[k, i] for i in range(PARTS)], axis=1)
        latent = latent + parts.astype(F32) * factor
    latent = latent / total

    high = latent.astype(BF16).astype(F32)
    both = jnp.concatenate([high, latent - high], axis=0)
    wide = jnp.concatenate([both] * GROUP, axis=1)
    row_of = lax.rem(lax.broadcasted_iota(jnp.int32, wide.shape, 0), GROUP)
    col_of = lax.div(lax.broadcasted_iota(jnp.int32, wide.shape, 1), LATENT)
    wide = jnp.where(row_of == col_of, wide, 0.0).astype(BF16)
    projected = dot(wide, wuv[...], ((1,), (0,)))
    out_ref[0] = (projected[:GROUP] + projected[GROUP:]).astype(BF16)

    for j in range(1, 8):
        send_stats(j).wait_send()
        for i in range(PARTS):
            send_part(j, i).wait_send()
    for j in range(1, 5):
        send_queries(j).wait_send()

    @pl.when(others_piece)
    def _():
        send_queries(0).wait_send()
        send_stats(0).wait_send()
        for i in range(PARTS):
            send_part(0, i).wait_send()

    for g in range(4):
        for c in range(2):
            forward(c, g).wait_send()

    @pl.when(relays)
    def _():
        for g in range(4):
            for c in range(2):
                for copy in spread(c, g):
                    copy.wait_send()

    @pl.when(passes)
    def _():
        for g in range(4):
            for c in range(2):
                pass_on(c, g).wait_send()

    for copy in swaps + news + back + [back_s]:
        copy.wait_send()


def shards(queries, new_latent, cache, lengths, w_uk, w_uv):
    anywhere = pl.BlockSpec(memory_space=pltpu.HBM)
    dma = pltpu.SemaphoreType.DMA
    return pl.pallas_call(
        kernel,
        out_shape=jax.ShapeDtypeStruct((1, GROUP, VDIM), BF16),
        in_specs=[
            anywhere,
            anywhere,
            anywhere,
            anywhere,
            anywhere,
            anywhere,
        ],
        out_specs=pl.BlockSpec(memory_space=pltpu.VMEM),
        scratch_shapes=[
            pltpu.SMEM((SEQS,), jnp.int32),
            pltpu.VMEM((GROUP * NOPE, LATENT), BF16),
            pltpu.VMEM((GROUP * LATENT, VDIM), BF16),
            pltpu.VMEM((GROUP, NOPE + ROPE), BF16),
            pltpu.VMEM((SPEC, 1, WIDTH), BF16),
            pltpu.VMEM((WIDTH, 4 * SLOTS), BF16),
            pltpu.VMEM((4 * SLOTS, LATENT + 128), BF16),
            pltpu.VMEM((PACKED, 128), BF16),
            pltpu.VMEM((4, 4, PACKED, 128), BF16),
            pltpu.VMEM((PARTS, PART, 2 * HEADS), BF16),
            pltpu.VMEM((2, 2 * HEADS), F32),
            pltpu.VMEM((PARTS, PART, 2 * HEADS), BF16),
            pltpu.VMEM((2, 2 * HEADS), F32),
            pltpu.VMEM((PARTS, 2 * HEADS, PART), BF16),
            pltpu.VMEM((2, 2 * HEADS), F32),
            pltpu.VMEM((8, PARTS, GROUP, PART), BF16),
            pltpu.VMEM((8, 2, 2 * HEADS), F32),
            dma((6,)),
            dma((3,)),
            dma((4,)),
            dma((3,)),
            dma((4,)),
            dma((8,)),
            dma((8,)),
            dma((2, 8)),
            dma((8,)),
            dma((8,)),
            dma((PARTS,)),
            dma((PARTS,)),
            dma,
            dma,
            dma((8, PARTS)),
            dma((8, PARTS)),
            dma((8,)),
            dma((8,)),
        ],
        compiler_params=pltpu.CompilerParams(
            collective_id=0, has_side_effects=True, vmem_limit_bytes=40 << 20
        ),
    )(*[
        pltpu.with_memory_space_constraint(array, pltpu.HBM)
        for array in (
            queries,
            new_latent,
            jnp.swapaxes(cache, 1, 2),
            lengths,
            w_uk.reshape(GROUP * NOPE, LATENT),
            w_uv.reshape(GROUP * LATENT, VDIM),
        )
    ])


def solution(mesh):
    return jax.shard_map(
        shards,
        mesh=mesh,
        in_specs=(
            P("seq", "head", None),
            P("seq", None),
            P("head", "seq", None),
            P(),
            P("head", None, None),
            P("head", None, None),
        ),
        out_specs=P("seq", "head", None),
        check_vma=False,
    )
```

```python
import jax
import jax.numpy as jnp
from jax import lax
from jax.experimental import pallas as pl
from jax.experimental.pallas import tpu as pltpu
from jax.sharding import PartitionSpec as P

NOPE = 128
ROPE = 64
LATENT = 512
WIDTH = LATENT + ROPE
VDIM = 128
SPEC = 4
GROUP = 16
HEADS = 64
PARTS = 2
PART = LATENT // PARTS
SEQS = 16
SLOTS = 128
NEG = -1e30
PACKED = GROUP * WIDTH // 128
SCALE = (NOPE + ROPE) ** -0.5
MESH = pl.DeviceIdType.MESH
F32 = jnp.float32
BF16 = jnp.bfloat16


def dot(a, b, dims):
    return lax.dot_general(a, b, (dims, ((), ())), preferred_element_type=F32)


def kernel(
    q_hbm, nl_hbm, cache_hbm, len_hbm, wuk_hbm, wuv_hbm, out_ref,
    len_ref, wuk, wuv, q_in, nl, kt, kv, q_own, q_all, o_out, s_out, o_in, s_in,
    r_out, t_out, r_in, t_in,
    local_sem, swap_send, swap_recv, nl_send, nl_recv, a_send, a_recv, f_send, b_send, b_recv,
    o_send, o_recv, s_send, s_recv, r_send, r_recv, t_send, t_recv,
):
    seq, head = lax.axis_index("seq"), lax.axis_index("head")
    core = lax.rem(seq, 2)
    x = lax.rem(lax.div(seq, 2), 4)
    y = lax.rem(lax.div(seq, 8), 4)
    zhi = lax.div(seq, 32)

    def at(zhi_, y_, x_, core_):
        return ((zhi_ * 4 + y_) * 4 + x_) * 2 + core_

    to_head, to_core = zhi * 2 + lax.div(y, 2), lax.rem(y, 2)
    plane = zhi * 4 + y
    from_zhi, from_y = lax.div(head, 2), lax.rem(head, 2) * 2 + core
    own_piece = (to_head == head) & (to_core == core)
    others_piece = jnp.logical_not(own_piece)

    def worker(j):
        zhi_ = zhi if j < 4 else 1 - zhi
        return at(zhi_, lax.rem(y + j % 4, 4), x, to_core), to_head

    def owner(j):
        return at(from_zhi, from_y, x, lax.rem(core + j // 4, 2)), lax.rem(head + j % 4, 4)

    odd = lax.rem(x, 2)
    relays = (from_zhi != zhi) & (from_y == y)
    along_y = [(at(zhi, lax.rem(y + d, 4), x, core), head) for d in (2, 1, 3)]
    near_x, pair_x, upper = x + 1 - 2 * odd, 3 - x, lax.div(x, 2)
    twin = (at(zhi, y, x, 1 - core), head)
    beside = (at(zhi, y, near_x, core), head)
    mates = [twin, beside, (at(zhi, y, near_x, 1 - core), head)]
    pair = [(at(zhi, y, pair_x, core), head), (at(zhi, y, pair_x, 1 - core), head)]

    barrier = pltpu.get_barrier_semaphore()

    def greet(device):
        pl.semaphore_signal(barrier, inc=1, device_id=device, device_id_type=MESH)

    @pl.when((from_zhi == zhi) | (from_y == y))
    def _():
        for j in range(7, 0, -1):
            greet(owner(j))

        @pl.when(others_piece)
        def _():
            greet(owner(0))

    for device in mates + pair + along_y:
        greet(device)

    def remote(src, dst, send, recv, device):
        return pltpu.make_async_remote_copy(
            src_ref=src, dst_ref=dst, send_sem=send, recv_sem=recv,
            device_id=device, device_id_type=MESH,
        )

    def slots(block):
        return kt.at[:, pl.ds(pl.multiple_of(block * SLOTS, SLOTS), SLOTS)]

    token = lax.rem(seq, SPEC)

    load_q = pltpu.make_async_copy(q_hbm.at[0], q_in, local_sem.at[0])
    load_wuk = pltpu.make_async_copy(wuk_hbm, wuk, local_sem.at[1])
    load_nl = pltpu.make_async_copy(nl_hbm, nl.at[token], local_sem.at[2])
    load_kt = pltpu.make_async_copy(
        cache_hbm.at[2 * core + upper], slots(core), local_sem.at[3]
    )
    load_wuv = pltpu.make_async_copy(wuv_hbm, wuv, local_sem.at[4])
    load_q.start()
    load_wuk.start()
    load_nl.start()
    load_kt.start()
    load_wuv.start()
    load_len = pltpu.make_async_copy(len_hbm, len_ref, local_sem.at[5])
    load_len.start()

    load_q.wait()
    q = q_in[...]
    row_of = lax.broadcasted_iota(jnp.int32, (GROUP, GROUP * NOPE), 0)
    col_of = lax.broadcasted_iota(jnp.int32, (GROUP, GROUP * NOPE), 1)
    diagonal = jnp.concatenate([q[:, :NOPE].astype(F32)] * GROUP, axis=1)
    diagonal = jnp.where(lax.div(col_of, NOPE) == row_of, diagonal, 0.0).astype(BF16)
    load_wuk.wait()
    absorbed = dot(diagonal, wuk[...], ((1,), (0,)))
    for i in range(4):
        q_own[GROUP * i : GROUP * (i + 1)] = absorbed[:, 128 * i : 128 * (i + 1)].astype(BF16)
    rope = q[:, NOPE:].astype(F32)
    rope = jnp.concatenate([rope[: GROUP // 2], rope[GROUP // 2 :]], axis=1)
    q_own[4 * GROUP :] = rope.astype(BF16)

    pl.semaphore_wait(barrier, jnp.where(own_piece, 12, 13))

    my_slot = core * 4 + head

    def rows_of(x_, core_, head_):
        return q_all.at[2 * lax.rem(x_, 2) + core_, head_]

    my_place = rows_of(x, core, head)

    def send_queries(j):
        return remote(q_own, my_place, a_send.at[j], a_recv.at[my_slot], worker(j))

    for j in (4, 1, 3, 2):
        send_queries(j).start()

    @pl.when(own_piece)
    def _():
        pltpu.make_async_copy(q_own, my_place, a_recv.at[my_slot]).start()

    @pl.when(others_piece)
    def _():
        send_queries(0).start()

    swaps = [
        remote(cache_hbm.at[2 * (1 - core) + upper], slots(core),
               swap_send.at[0], swap_recv.at[core], twin),
        remote(cache_hbm.at[2 * core + 1 - upper], slots(2 + core),
               swap_send.at[1], swap_recv.at[2 + core], pair[0]),
        remote(cache_hbm.at[2 * (1 - core) + 1 - upper], slots(2 + core),
               swap_send.at[2], swap_recv.at[2 + core], pair[1]),
    ]
    load_nl.wait()
    news = [
        remote(nl.at[token], nl.at[token], nl_send.at[k], nl_recv.at[token], mates[k])
        for k in range(3)
    ]

    for copy in swaps + news:
        copy.start()

    def forward(c, g):
        place = rows_of(x, c, g)
        return remote(place, place, b_send.at[4 * c + g], b_recv.at[4 * c + g], beside)

    def spread(c, g):
        place = rows_of(x, c, g)
        return [
            remote(place, place, f_send.at[d, 4 * c + g], a_recv.at[4 * c + g], along_y[d])
            for d in range(3)
        ]

    for k in range(4):
        g = jnp.where(zhi == 0, k, 3 - k)
        for c in range(2):
            pltpu.make_async_copy(q_own, rows_of(x, c, g), a_recv.at[4 * c + g]).wait()

            @pl.when(relays)
            def _():
                for copy in spread(c, g):
                    copy.start()

            forward(c, g).start()

    load_kt.wait()
    for block in (1 - core, 2, 3):
        pltpu.make_async_copy(cache_hbm.at[0], slots(block), swap_recv.at[block]).wait()
    kv[:, :LATENT] = kt[:LATENT].T
    kv[:, LATENT:] = jnp.concatenate([kt[LATENT:], kt[LATENT:]], axis=0).T

    chip = lax.div(seq, 2)
    load_len.wait()
    length = len_ref[4 * head + 2 * core + upper]
    step = (3 - 2 * x) * (2 * SLOTS)

    def partial_of(x_):
        pieces = pl.ds(2 * lax.rem(x_, 2), 2)
        queries = [
            q_all[pieces, :, GROUP * i : GROUP * (i + 1)].reshape(2 * HEADS, 128)
            for i in range(4)
        ]
        ropes = q_all[pieces, :, 4 * GROUP :].astype(F32)
        first = lax.broadcasted_iota(jnp.int32, ropes.shape, 3) < ROPE
        ropes = jnp.concatenate(
            [jnp.where(first, ropes, 0.0), jnp.where(first, 0.0, ropes)], axis=2
        )
        queries.append(ropes.reshape(2 * HEADS, 128).astype(BF16))
        queries = jnp.concatenate(queries, axis=1)
        scores = dot(kv[...], queries, ((1,), (1,))) * SCALE
        slot = lax.broadcasted_iota(jnp.int32, scores.shape, 0)
        position = chip * (2 * SLOTS) + jnp.where(
            slot < 2 * SLOTS, slot, slot - 2 * SLOTS + step
        )
        visible = position < length
        top = jnp.max(jnp.where(visible, scores, NEG), axis=0, keepdims=True)
        p = jnp.where(visible, jnp.exp(scores - top), 0.0)
        total = jnp.sum(p, axis=0, keepdims=True)
        return top, total, p.astype(BF16)

    def weighted_of(p, j):
        return dot(kt[PART * j : PART * (j + 1)], p, ((1,), (0,)))

    def put_stats(ref, top, total):
        ref[0:1] = top
        ref[1:2] = total

    for k in range(4):
        for c in range(2):
            pltpu.make_async_copy(q_own, rows_of(near_x, c, k), b_recv.at[4 * c + k]).wait()
    top_1, total_1, p_1 = partial_of(near_x)
    put_stats(s_out, top_1, total_1)
    back_s = remote(s_out, s_in, s_send, s_recv, beside)
    back_s.start()
    back = []
    for j in range(PARTS):
        o_out[j] = weighted_of(p_1, j).astype(BF16)
        back.append(remote(o_out.at[j], o_in.at[j], o_send.at[j], o_recv.at[j], beside))
        back[j].start()
    top_0, total_0, p_0 = partial_of(x)
    weighted_0 = [weighted_of(p_0, j) for j in range(PARTS)]

    back_s.wait_recv()
    top_1, total_1 = s_in[0:1], s_in[1:2]
    top = jnp.maximum(top_0, top_1)
    factor_0, factor_1 = jnp.exp(top_0 - top), jnp.exp(top_1 - top)
    put_stats(t_out, top, total_0 * factor_0 + total_1 * factor_1)

    def place_of(j):
        core_, head_ = lax.rem(core + j // 4, 2), lax.rem(head + j % 4, 4)
        return pl.ds(pl.multiple_of(HEADS * core_ + GROUP * head_, GROUP), GROUP)

    def send_stats(j):
        return remote(t_out, t_in.at[plane], t_send.at[j], t_recv.at[plane], owner(j))

    def send_part(j, i):
        return remote(
            r_out.at[i, place_of(j)], r_in.at[plane, i], r_send.at[j, i],
            r_recv.at[plane, i], owner(j),
        )

    def to_owners(send, keep):
        for j in range(7, 0, -1):
            send(j).start()

        @pl.when(own_piece)
        def _():
            keep().start()

        @pl.when(others_piece)
        def _():
            send(0).start()

    to_owners(
        send_stats,
        lambda: pltpu.make_async_copy(t_out, t_in.at[plane], t_recv.at[plane]),
    )
    for i in range(PARTS):
        back[i].wait_recv()
        merged = weighted_0[i] * factor_0 + o_in[i].astype(F32) * factor_1
        r_out[i] = merged.T.astype(BF16)
        to_owners(
            lambda j, i=i: send_part(j, i),
            lambda i=i: pltpu.make_async_copy(
                r_out.at[i, place_of(0)], r_in.at[plane, i], r_recv.at[plane, i]
            ),
        )

    for k in range(1, 4):
        other_token = lax.rem(token + k, SPEC)
        pltpu.make_async_copy(nl.at[token], nl.at[other_token], nl_recv.at[other_token]).wait()
    mine = [q_own[GROUP * i : GROUP * (i + 1)].astype(F32) for i in range(4)]
    mine = jnp.concatenate(mine + [q_in[:, NOPE:].astype(F32)], axis=1)
    fresh, keys = [], []
    for i in range(SPEC):
        key = nl[i].astype(F32)
        score = jnp.sum(mine * key, axis=1, keepdims=True) * SCALE
        fresh.append(jnp.where(i <= token, score, NEG))
        keys.append(key[:, :LATENT])
    f_top = jnp.maximum(jnp.maximum(fresh[0], fresh[1]), jnp.maximum(fresh[2], fresh[3]))
    f_total, f_weighted = 0.0, 0.0
    for i in range(SPEC):
        p = jnp.where(i <= token, jnp.exp(fresh[i] - f_top), 0.0)
        f_total = f_total + p
        f_weighted = f_weighted + p.astype(BF16).astype(F32) * keys[i]
    load_wuv.wait()

    for k in range(8):
        pltpu.make_async_copy(t_in.at[k], t_in.at[k], t_recv.at[k]).wait()
        for i in range(PARTS):
            pltpu.make_async_copy(r_in.at[k, i], r_in.at[k, i], r_recv.at[k, i]).wait()
    lane = lax.broadcasted_iota(jnp.int32, (GROUP, 2 * HEADS), 1)
    mine_lane = lane == (
        HEADS * core + GROUP * head + lax.broadcasted_iota(jnp.int32, (GROUP, 2 * HEADS), 0)
    )

    def column(row):
        return jnp.sum(jnp.where(mine_lane, row, 0.0), axis=1, keepdims=True)

    tops = [column(t_in[k, 0:1]) for k in range(8)]
    top = f_top
    for t in tops:
        top = jnp.maximum(top, t)
    f_factor = jnp.exp(f_top - top)
    total = f_total * f_factor
    latent = f_weighted * f_factor
    for k in range(8):
        factor = jnp.exp(tops[k] - top)
        total = total + column(t_in[k, 1:2]) * factor
        parts = jnp.concatenate([r_in[k, i] for i in range(PARTS)], axis=1)
        latent = latent + parts.astype(F32) * factor
    latent = latent / total

    high = latent.astype(BF16).astype(F32)
    both = jnp.concatenate([high, latent - high], axis=0)
    wide = jnp.concatenate([both] * GROUP, axis=1)
    row_of = lax.rem(lax.broadcasted_iota(jnp.int32, wide.shape, 0), GROUP)
    col_of = lax.div(lax.broadcasted_iota(jnp.int32, wide.shape, 1), LATENT)
    wide = jnp.where(row_of == col_of, wide, 0.0).astype(BF16)
    projected = dot(wide, wuv[...], ((1,), (0,)))
    out_ref[0] = (projected[:GROUP] + projected[GROUP:]).astype(BF16)

    for j in range(1, 8):
        send_stats(j).wait_send()
        for i in range(PARTS):
            send_part(j, i).wait_send()
    for j in range(1, 5):
        send_queries(j).wait_send()

    @pl.when(others_piece)
    def _():
        send_queries(0).wait_send()
        send_stats(0).wait_send()
        for i in range(PARTS):
            send_part(0, i).wait_send()

    for g in range(4):
        for c in range(2):
            forward(c, g).wait_send()

    @pl.when(relays)
    def _():
        for g in range(4):
            for c in range(2):
                for copy in spread(c, g):
                    copy.wait_send()

    for copy in swaps + news + back + [back_s]:
        copy.wait_send()


def shards(queries, new_latent, cache, lengths, w_uk, w_uv):
    anywhere = pl.BlockSpec(memory_space=pltpu.HBM)
    dma = pltpu.SemaphoreType.DMA
    return pl.pallas_call(
        kernel,
        out_shape=jax.ShapeDtypeStruct((1, GROUP, VDIM), BF16),
        in_specs=[
            anywhere,
            anywhere,
            anywhere,
            anywhere,
            anywhere,
            anywhere,
        ],
        out_specs=pl.BlockSpec(memory_space=pltpu.VMEM),
        scratch_shapes=[
            pltpu.SMEM((SEQS,), jnp.int32),
            pltpu.VMEM((GROUP * NOPE, LATENT), BF16),
            pltpu.VMEM((GROUP * LATENT, VDIM), BF16),
            pltpu.VMEM((GROUP, NOPE + ROPE), BF16),
            pltpu.VMEM((SPEC, 1, WIDTH), BF16),
            pltpu.VMEM((WIDTH, 4 * SLOTS), BF16),
            pltpu.VMEM((4 * SLOTS, LATENT + 128), BF16),
            pltpu.VMEM((PACKED, 128), BF16),
            pltpu.VMEM((4, 4, PACKED, 128), BF16),
            pltpu.VMEM((PARTS, PART, 2 * HEADS), BF16),
            pltpu.VMEM((2, 2 * HEADS), F32),
            pltpu.VMEM((PARTS, PART, 2 * HEADS), BF16),
            pltpu.VMEM((2, 2 * HEADS), F32),
            pltpu.VMEM((PARTS, 2 * HEADS, PART), BF16),
            pltpu.VMEM((2, 2 * HEADS), F32),
            pltpu.VMEM((8, PARTS, GROUP, PART), BF16),
            pltpu.VMEM((8, 2, 2 * HEADS), F32),
            dma((6,)),
            dma((3,)),
            dma((4,)),
            dma((3,)),
            dma((4,)),
            dma((8,)),
            dma((8,)),
            dma((3, 8)),
            dma((8,)),
            dma((8,)),
            dma((PARTS,)),
            dma((PARTS,)),
            dma,
            dma,
            dma((8, PARTS)),
            dma((8, PARTS)),
            dma((8,)),
            dma((8,)),
        ],
        compiler_params=pltpu.CompilerParams(
            collective_id=0, has_side_effects=True, vmem_limit_bytes=40 << 20
        ),
    )(*[
        pltpu.with_memory_space_constraint(array, pltpu.HBM)
        for array in (
            queries,
            new_latent,
            jnp.swapaxes(cache, 1, 2),
            lengths,
            w_uk.reshape(GROUP * NOPE, LATENT),
            w_uv.reshape(GROUP * LATENT, VDIM),
        )
    ])


def solution(mesh):
    return jax.shard_map(
        shards,
        mesh=mesh,
        in_specs=(
            P("seq", "head", None),
            P("seq", None),
            P("head", "seq", None),
            P(),
            P("head", None, None),
            P("head", None, None),
        ),
        out_specs=P("seq", "head", None),
        check_vma=False,
    )
```
